512 devices in a mesh: ctx: 64 (over y, z_hi, core), rep: 8 (over z_lo, x).
Axes of the slice: x: 4, y: 8, z: 8 (z_hi: 4, z_lo: 2; z = z_hi * 2 + z_lo), core: 2. Of those that a mesh axis runs over, the one named last changes fastest.
Arguments:
- hidden_in: bfloat16 [2, 64, 2, 32, 4096], P(None, 'ctx'), may hold values from -6 to 6
- norm_gain: bfloat16 [4096], replicated, may hold values from 0.3984375 to 1.59375
- w_query: bfloat16 [4096, 4096], P('ctx', 'rep')
- key_matrix: bfloat16 [4096, 512], P('ctx'), may hold values from -0.09375 to 0.09375
- value_matrix: bfloat16 [4096, 512], P('ctx'), may hold values from -0.09375 to 0.09375
- w_out: bfloat16 [4096, 4096], P('rep', 'ctx'), may hold values from -0.1875 to 0.1875
- prompt_len: int32 [2], replicated, may hold values from 3276 to 4096, as said below
- pair_of_device: int32 [2, 64], replicated, may hold values from 0 to 63, each once within a row
- cache_pages: bfloat16 [64, 8, 16, 16, 1024], P('ctx', 'rep'), may hold values from -6 to 6
- move_page: int32 [64, 8, 2], P('ctx', 'rep'), may hold values from 0 to 13, as said below
- move_dest: int32 [64, 8, 2], P('ctx', 'rep'), may hold values from 0 to 7, as said below
- move_slot: int32 [64, 8, 2], P('ctx', 'rep'), may hold values from 14 to 15, as said below
Outputs:
- attn_out: bfloat16 [2, 64, 2, 32, 4096], P(None, 'ctx', None, None, 'rep')
- new_cache: bfloat16 [64, 8, 16, 16, 1024], P('ctx', 'rep')
The draws below stay inside these ranges and needn't reach their ends.
Inputs may be any that keep to these rules, and one draw needn't show every extreme that they name: `prompt_len`: one of the two prompts has exactly 4096 tokens. `move_page`: the 2 pages that leave one device are different, and none lies in slots 16 - 2 to 15. `move_dest`: within each index of ctx, every pair of an index of rep and a slot of 14 to 15 receives exactly one page; a page may stay on its own device. `move_slot`: see move_dest.
All inputs are finite; a program needn't handle non-finite values.
Results may differ from the reference program's by a relative error of at most 0.019.
The reference program's roundings to bfloat16 on the way count: a program that leaves them out, or rounds other values in their place, can miss the bound.
Values may be sent and summed in bfloat16 or wider, within the bound.
No kernel may reach another device: no remote copies, remote signals or barrier semaphores. Data moves between devices by JAX's collectives and lax.ppermute only.
A program may use at most 64 MiB of HBM per device.

```python
import math
import jax
import jax.numpy as jnp
from jax import lax

MODEL_WIDTH = 4096
QUERY_HEADS = 32
KEY_VALUE_HEADS = 4
HEAD_SIZE = 128
BLK = 32
PTOK = 16
PAGES = 16
MOVES = 2
PROMPT_SLOTS = 4096
HQD = 4
PW = 1024
N_CTX = 64
N_REP = 8


def migration_plan(key):
    cycle = PROMPT_SLOTS // (2 * BLK)
    groups = QUERY_HEADS // HQD
    keep = PAGES - MOVES
    page_key, dest_key = jax.random.split(jax.random.fold_in(key, 4242))
    raw = jax.random.randint(page_key, (cycle, groups, keep), 0, 1 << 20) * keep + jnp.arange(keep, dtype=jnp.int32)
    chosen = jnp.argsort(raw, axis=-1)[..., :MOVES].astype(jnp.int32)
    slots = groups * MOVES
    raw_dest = jax.random.randint(dest_key, (cycle, slots), 0, 1 << 20) * slots + jnp.arange(slots, dtype=jnp.int32)
    target = jnp.argsort(raw_dest, axis=-1).astype(jnp.int32).reshape(cycle, groups, MOVES)
    return (chosen, (target // MOVES).astype(jnp.int32), (keep + target % MOVES).astype(jnp.int32))


def draw_move_page(key, part):
    return migration_plan(key)[0]


def draw_move_dest(key, part):
    return migration_plan(key)[1]


def draw_move_slot(key, part):
    return migration_plan(key)[2]


def draw_prompt_len(key, part):
    first_key, second_key = jax.random.split(jax.random.fold_in(key, 11))
    short = jax.random.randint(first_key, (), 4 * PROMPT_SLOTS // 5, PROMPT_SLOTS + 1).astype(jnp.int32)
    flip = jax.random.randint(second_key, (), 0, 2)
    full = jnp.array(PROMPT_SLOTS, dtype=jnp.int32)
    return jnp.where(flip == 0, jnp.stack([full, short]), jnp.stack([short, full])).astype(jnp.int32)


def draw_w_query(key, part):
    base = jax.random.normal(jax.random.fold_in(key, 5), (MODEL_WIDTH, QUERY_HEADS * HEAD_SIZE), jnp.float32) * MODEL_WIDTH ** (-0.5)
    base = base * 2.0
    return base.astype(jnp.bfloat16)


def steps_of(stream_key, extent, shards, smallest, high):
    loudness, own = 1.0, jax.random.fold_in(stream_key, 6)
    for position, parts in shards:
        heights = jnp.exp(jax.random.uniform(jax.random.fold_in(own, position), (parts,), jnp.float32, smallest / len(shards), high / len(shards)))
        loudness = loudness * jnp.repeat(heights, extent[position] // parts).reshape([-1 if axis == position else 1 for axis in range(len(extent))])
    return loudness


def scatter_about(own_key, dims, width, reach, cuts=(), kind=jnp.bfloat16):
    level = steps_of(own_key, dims, cuts, -0.22, 0.18) if cuts else 1.0
    entries = jax.random.normal(own_key, dims, jnp.float32) * width * level
    return jnp.minimum(jnp.maximum(entries, -reach), reach).astype(kind)


def setup_inputs(seed: int = 0) -> dict:
    key_list = jax.random.split(jax.random.key(seed), 13)
    hidden_in = scatter_about(key_list[0], (2, N_CTX, 2, BLK, MODEL_WIDTH), 1.0, 6.0, ((1, 64),))
    norm_gain = jnp.clip(1.0 + 0.12 * jax.random.normal(key_list[1], (MODEL_WIDTH,), jnp.float32), 0.3984375, 1.59375).astype(jnp.bfloat16)
    w_query = draw_w_query(jax.random.fold_in(key_list[12], 71), 0)
    key_matrix = scatter_about(key_list[3], (MODEL_WIDTH, KEY_VALUE_HEADS * HEAD_SIZE), MODEL_WIDTH ** -0.5, 0.09375, ((0, 64),))
    value_matrix = scatter_about(key_list[4], (MODEL_WIDTH, KEY_VALUE_HEADS * HEAD_SIZE), MODEL_WIDTH ** -0.5, 0.09375, ((0, 64),))
    w_out = scatter_about(key_list[5], (QUERY_HEADS * HEAD_SIZE, MODEL_WIDTH), (2.0 * (QUERY_HEADS * HEAD_SIZE) ** -0.5), 0.1875, ((0, 8), (1, 64)))
    prompt_len = draw_prompt_len(jax.random.fold_in(key_list[12], 71), 0)
    pair_of_device = jax.vmap(lambda own: jax.random.permutation(own, N_CTX))(jax.random.split(key_list[7], 2)).reshape((2, N_CTX)).astype(jnp.int32)
    cache_pages = scatter_about(key_list[8], (N_CTX, N_REP, PAGES, PTOK, PW), 1.0, 6.0, ((0, 64), (1, 8)))
    move_page = draw_move_page(jax.random.fold_in(key_list[12], 71), 0)
    move_dest = draw_move_dest(jax.random.fold_in(key_list[12], 71), 0)
    move_slot = draw_move_slot(jax.random.fold_in(key_list[12], 71), 0)
    return dict(hidden_in=hidden_in, norm_gain=norm_gain, w_query=w_query, key_matrix=key_matrix, value_matrix=value_matrix, w_out=w_out, prompt_len=prompt_len, pair_of_device=pair_of_device, cache_pages=cache_pages, move_page=move_page, move_dest=move_dest, move_slot=move_slot)


rope_base = 5000000.0
neg_fill = -1e+30

def rope_tables(positions):
    half = HEAD_SIZE // 2
    steps_f = jnp.arange(half, dtype=jnp.float32) * (2.0 / HEAD_SIZE)
    freq = jnp.exp(-steps_f * math.log(rope_base))
    angle = positions.astype(jnp.float32)[:, None] * freq[None, :]
    return (jnp.cos(angle), jnp.sin(angle))

def apply_rotation(values, cosine_table, sine_table):
    half = values.shape[-1] // 2
    first = values[..., :half]
    second = values[..., half:]
    cosine_table = cosine_table[:, None, :]
    sine_table = sine_table[:, None, :]
    return jnp.concatenate([first * cosine_table - second * sine_table, second * cosine_table + first * sine_table], axis=-1)

def reference(hidden_in, norm_gain, w_query, key_matrix, value_matrix, w_out, prompt_len, pair_of_device, cache_pages, move_page, move_dest, move_slot):
    hidden = hidden_in.astype(jnp.float32)
    scale = lax.rsqrt(lax.optimization_barrier(jnp.mean(hidden * hidden, axis=-1, keepdims=True)) + 1e-05)
    normalized_input = (hidden * scale * norm_gain.astype(jnp.float32)).astype(jnp.bfloat16).reshape(-1, MODEL_WIDTH)
    query = jnp.dot(normalized_input, w_query, preferred_element_type=jnp.float32)
    key_projected = jnp.dot(normalized_input, key_matrix, preferred_element_type=jnp.float32)
    value_projected = jnp.dot(normalized_input, value_matrix, preferred_element_type=jnp.float32).astype(jnp.bfloat16).reshape(2, PROMPT_SLOTS, KEY_VALUE_HEADS, HEAD_SIZE)
    blocks = jnp.stack([pair_of_device, 2 * N_CTX - 1 - pair_of_device], axis=2)
    positions = (blocks[..., None] * BLK + jnp.arange(BLK, dtype=jnp.int32)).reshape(2, PROMPT_SLOTS)
    cosine_table, sine_table = rope_tables(positions.reshape(-1))
    query = apply_rotation(query.reshape(-1, QUERY_HEADS, HEAD_SIZE), cosine_table, sine_table).astype(jnp.bfloat16).reshape(2, PROMPT_SLOTS, QUERY_HEADS, HEAD_SIZE)
    key_projected = apply_rotation(key_projected.reshape(-1, KEY_VALUE_HEADS, HEAD_SIZE), cosine_table, sine_table).astype(jnp.bfloat16).reshape(2, PROMPT_SLOTS, KEY_VALUE_HEADS, HEAD_SIZE)
    head_group = QUERY_HEADS // KEY_VALUE_HEADS
    score_scale = HEAD_SIZE ** (-0.5)

    def one_head(index):
        prompt = index // QUERY_HEADS
        head = index % QUERY_HEADS
        q_rows = lax.dynamic_index_in_dim(lax.dynamic_index_in_dim(query, prompt, 0, False), head, 1, False)
        k_rows = lax.dynamic_index_in_dim(lax.dynamic_index_in_dim(key_projected, prompt, 0, False), head // head_group, 1, False)
        v_rows = lax.dynamic_index_in_dim(lax.dynamic_index_in_dim(value_projected, prompt, 0, False), head // head_group, 1, False)
        pos = lax.dynamic_index_in_dim(positions, prompt, 0, False)
        length = lax.dynamic_index_in_dim(prompt_len, prompt, 0, False)
        allowed = (pos[None, :] <= pos[:, None]) & (pos[:, None] < length)
        scores = jnp.dot(q_rows, k_rows.T, preferred_element_type=jnp.float32) * score_scale
        top = lax.optimization_barrier(jnp.max(jnp.where(allowed, scores, neg_fill), axis=-1, keepdims=True))
        weights = jnp.where(allowed, jnp.exp(scores - top), 0.0)
        total = jnp.maximum(lax.optimization_barrier(jnp.sum(weights, axis=-1, keepdims=True)), 1.0)
        return jnp.dot(weights.astype(jnp.bfloat16), v_rows, preferred_element_type=jnp.float32) / total
    heads = lax.map(one_head, jnp.arange(2 * QUERY_HEADS, dtype=jnp.int32))
    context = heads.reshape(2, QUERY_HEADS, PROMPT_SLOTS, HEAD_SIZE).transpose(0, 2, 1, 3).reshape(2 * PROMPT_SLOTS, QUERY_HEADS * HEAD_SIZE).astype(jnp.bfloat16)
    per_group = QUERY_HEADS * HEAD_SIZE // N_REP
    summed = jnp.zeros((2 * PROMPT_SLOTS, MODEL_WIDTH), jnp.float32)
    for rank in range(N_REP):
        term = jnp.dot(context[:, rank * per_group:(rank + 1) * per_group], w_out[rank * per_group:(rank + 1) * per_group], preferred_element_type=jnp.float32)
        rounded = lax.optimization_barrier(term.astype(jnp.bfloat16))
        summed = summed + rounded.astype(jnp.float32)
    attn_out = summed.astype(jnp.bfloat16).reshape(2, N_CTX, 2, BLK, MODEL_WIDTH)
    leaving = jnp.take_along_axis(cache_pages, move_page[:, :, :, None, None], axis=2)
    gone = jnp.any(move_page[..., None] == jnp.arange(PAGES, dtype=jnp.int32), axis=2)
    kept = jnp.where(gone[:, :, :, None, None], jnp.zeros_like(cache_pages), cache_pages)
    cycle_index = jnp.broadcast_to(jnp.arange(N_CTX, dtype=jnp.int32)[:, None, None], move_dest.shape)
    new_cache = kept.at[cycle_index, move_dest, move_slot].set(leaving)
    return (attn_out, new_cache)
```

```python
import math

import jax
import jax.numpy as jnp
from jax import lax
from jax.experimental import pallas as pl
from jax.experimental.pallas import tpu as pltpu
from jax.sharding import Mesh
from jax.sharding import PartitionSpec as P

HEAD_SIZE = 128
HEADS_PER_KV = 8

CTX = ("y", "zh", "core")
REP = ("zl", "x")
CHIPS = ("y", "zh")

rope_base = 5000000.0
neg_fill = -1e30


def rope_tables(positions):
    half = HEAD_SIZE // 2
    steps_f = jnp.arange(half, dtype=jnp.float32) * (2.0 / HEAD_SIZE)
    freq = jnp.exp(-steps_f * math.log(rope_base))
    angle = positions.astype(jnp.float32)[:, None] * freq[None, :]
    return (jnp.cos(angle), jnp.sin(angle))


def apply_rotation(values, cosine_table, sine_table):
    half = values.shape[-1] // 2
    first = values[..., :half]
    second = values[..., half:]
    cosine_table = cosine_table[:, None, :]
    sine_table = sine_table[:, None, :]
    return jnp.concatenate(
        [first * cosine_table - second * sine_table, second * cosine_table + first * sine_table],
        axis=-1,
    )


def matmul(left, right):
    return jnp.dot(left, right, preferred_element_type=jnp.float32)


def spread(block, axes):
    size = lax.axis_size(axes)
    copies = jnp.broadcast_to(block[None], (size,) + block.shape)
    return lax.all_to_all(copies, axes, split_axis=0, concat_axis=0, tiled=True)


def gather_ring(block, axis):
    size = lax.axis_size(axis)
    place = lax.axis_index(axis)
    parts = [
        lax.ppermute(block, axis, [((i + hop) % size, i) for i in range(size)])
        for hop in range(1, size)
    ]
    parts = jnp.stack(parts + [block])
    return lax.dynamic_slice_in_dim(
        jnp.concatenate([parts, parts]), size - 1 - place, size, 0
    )


def swap_core(value):
    return lax.ppermute(value, "core", [(0, 1), (1, 0)])


def swap_x(value):
    return lax.ppermute(value, "x", [(i, i ^ 1) for i in range(lax.axis_size("x"))])


def attend_kernel(q_ref, near_ref, far_ref, qpos_ref, kpos_ref, out_ref):
    half = near_ref.shape[0]
    queries = q_ref[...]
    scores = []
    masks = []
    for part, ref in enumerate((near_ref, far_ref)):
        keys = ref[:, :HEAD_SIZE]
        raw = lax.dot_general(
            queries, keys, (((1,), (1,)), ((), ())), preferred_element_type=jnp.float32
        )
        raw = raw * HEAD_SIZE ** (-0.5)
        allowed = kpos_ref[:, part * half : (part + 1) * half] <= qpos_ref[...]
        scores.append(raw)
        masks.append(allowed)
    top = jnp.maximum(
        jnp.max(jnp.where(masks[0], scores[0], neg_fill), axis=-1, keepdims=True),
        jnp.max(jnp.where(masks[1], scores[1], neg_fill), axis=-1, keepdims=True),
    )
    total = jnp.zeros_like(top)
    acc = jnp.zeros(out_ref.shape, jnp.float32)
    for raw, allowed, ref in zip(scores, masks, (near_ref, far_ref)):
        weights = jnp.where(allowed, jnp.exp(raw - top), 0.0)
        total = total + jnp.sum(weights, axis=-1, keepdims=True)
        acc = acc + matmul(weights.astype(jnp.bfloat16), ref[:, HEAD_SIZE:])
    out_ref[...] = (acc / jnp.maximum(total, 1.0)).astype(jnp.bfloat16)


def attend(queries, near, far, qpos, kpos):
    rows, half = queries.shape[0], near.shape[0]
    tile = min(rows, 128)
    return pl.pallas_call(
        attend_kernel,
        grid=(rows // tile,),
        in_specs=[
            pl.BlockSpec((tile, HEAD_SIZE), lambda i: (i, 0)),
            pl.BlockSpec((half, 2 * HEAD_SIZE), lambda i: (0, 0)),
            pl.BlockSpec((half, 2 * HEAD_SIZE), lambda i: (0, 0)),
            pl.BlockSpec((tile, 1), lambda i: (i, 0)),
            pl.BlockSpec((1, 2 * half), lambda i: (0, 0)),
        ],
        out_specs=pl.BlockSpec((tile, HEAD_SIZE), lambda i: (i, 0)),
        out_shape=jax.ShapeDtypeStruct((rows, HEAD_SIZE), jnp.bfloat16),
        compiler_params=pltpu.CompilerParams(vmem_limit_bytes=40 << 20),
        name="attend",
    )(queries, near, far, qpos, kpos)


def pages_to_send(cache_pages, move_page, move_dest, move_slot):
    pages = cache_pages[0, 0]
    page_count = pages.shape[0]
    moves = move_page.shape[2]
    groups = lax.axis_size(REP)
    leave_ids = move_page[0, 0]
    dest_ids = move_dest[0, 0]
    slot_ids = move_slot[0, 0] - (page_count - moves)
    slots = jnp.arange(moves, dtype=jnp.int32)
    leaving = jnp.take(pages, leave_ids, axis=0)
    to_dest = dest_ids[None, :] == jnp.arange(groups, dtype=jnp.int32)[:, None]
    chosen = to_dest[:, None, :] & (slot_ids[None, :] == slots[:, None])[None]
    send = jnp.zeros((groups, moves) + pages.shape[1:], pages.dtype)
    for move in range(moves):
        send = jnp.where(chosen[:, :, move, None, None], leaving[move][None, None], send)
    return send


def settle_pages(cache_pages, move_page, arrived):
    pages = cache_pages[0, 0]
    page_count = pages.shape[0]
    moves = move_page.shape[2]
    leave_ids = move_page[0, 0]
    gone = jnp.any(leave_ids[:, None] == jnp.arange(page_count, dtype=jnp.int32)[None, :], axis=0)
    kept = jnp.where(gone[:, None, None], jnp.zeros_like(pages), pages)
    filled = jnp.sum(arrived.astype(jnp.float32), axis=0).astype(pages.dtype)
    new_pages = jnp.concatenate([kept[: page_count - moves], filled], axis=0)
    return new_pages.reshape(cache_pages.shape)


def on_device(
    hidden_in,
    norm_gain,
    w_query,
    key_matrix,
    value_matrix,
    w_out,
    prompt_len,
    pair_of_device,
    cache_pages,
    move_page,
    move_dest,
    move_slot,
):
    cycle = lax.axis_size(CTX)
    place = lax.axis_index(CTX)
    rank = lax.axis_index(REP)
    core = lax.axis_index("core")
    rows_y, rows_z = lax.axis_size("y"), lax.axis_size("zh")
    mine = lax.axis_index("x") % 2
    blk = hidden_in.shape[3]
    span = 2 * blk
    width = hidden_in.shape[4]
    piece = w_query.shape[0]
    heads_here = w_query.shape[1] // HEAD_SIZE
    kv_first = (rank * heads_here // HEADS_PER_KV) * HEAD_SIZE

    key_cols = lax.dynamic_slice_in_dim(key_matrix, kv_first, HEAD_SIZE, 1)
    value_cols = lax.dynamic_slice_in_dim(value_matrix, kv_first, HEAD_SIZE, 1)
    kv_near = spread(jnp.concatenate([key_cols, value_cols], axis=1), CHIPS)
    kv_near = kv_near.reshape(-1, 2 * HEAD_SIZE)
    kv_far = swap_core(kv_near)
    wq_near = gather_ring(w_query, "zh").reshape(rows_z * piece, -1)
    wq_near = lax.all_gather(wq_near, "y", axis=0, tiled=True)
    wo_near = gather_ring(w_out.T, "zh").reshape(rows_z * piece, -1)
    wo_near = lax.all_gather(wo_near, "y", axis=0, tiled=True)
    wq_far = swap_core(wq_near)

    hidden = hidden_in.reshape(2 * span, width).astype(jnp.float32)
    scale = lax.rsqrt(jnp.mean(hidden * hidden, axis=-1, keepdims=True) + 1e-05)
    normed = (hidden * scale * norm_gain.astype(jnp.float32)).astype(jnp.bfloat16)
    normed = normed.reshape(2 * span, rows_y * rows_z, 2, piece)
    even = normed[:, :, 0].reshape(2 * span, width // 2)
    odd = normed[:, :, 1].reshape(2 * span, width // 2)
    x_near = jnp.where(core == 0, even, odd)
    x_far = jnp.where(core == 0, odd, even)

    own_pair = lax.dynamic_slice_in_dim(pair_of_device, place, 1, 1)[:, 0]
    blocks = jnp.stack([own_pair, 2 * cycle - 1 - own_pair], axis=1)
    qpos = (blocks[:, :, None] * blk + jnp.arange(blk, dtype=jnp.int32)).reshape(2, span)
    cosine_table, sine_table = rope_tables(qpos.reshape(-1))

    def prompt_rows(table):
        return lax.dynamic_slice_in_dim(table, mine * span, span, 0)

    kv = matmul(prompt_rows(x_near), kv_near) + matmul(prompt_rows(x_far), kv_far)
    keys = apply_rotation(
        kv[:, None, :HEAD_SIZE], prompt_rows(cosine_table), prompt_rows(sine_table)
    )[:, 0]
    kv = jnp.concatenate([keys, kv[:, HEAD_SIZE:]], axis=1).astype(jnp.bfloat16)
    near = spread(kv, CHIPS).reshape(-1, 2 * HEAD_SIZE)
    arrived = lax.all_to_all(
        pages_to_send(cache_pages, move_page, move_dest, move_slot),
        REP,
        split_axis=0,
        concat_axis=0,
        tiled=True,
    )
    near, arrived = lax.optimization_barrier((near, arrived))
    far = swap_core(near)

    query = matmul(x_near, wq_near) + matmul(x_far, wq_far)
    query = apply_rotation(
        query.reshape(2 * span, heads_here, HEAD_SIZE), cosine_table, sine_table
    ).astype(jnp.bfloat16)
    query = query.reshape(2, span, heads_here * HEAD_SIZE)
    q_mine = lax.dynamic_index_in_dim(query, mine, 0, False)
    q_pair = swap_x(lax.dynamic_index_in_dim(query, 1 - mine, 0, False))

    q_pair, far, wo_near = lax.optimization_barrier((q_pair, far, wo_near))
    wo_far = swap_core(wo_near)

    pairs = lax.dynamic_index_in_dim(pair_of_device, mine, 0, False).reshape(-1, 2)
    pairs = jnp.where(core == 0, pairs, pairs[:, ::-1]).T.reshape(-1)
    kblocks = jnp.stack([pairs, 2 * cycle - 1 - pairs], axis=1)
    kpos = (kblocks[..., None] * blk + jnp.arange(blk, dtype=jnp.int32)).reshape(1, -1)
    my_qpos = lax.dynamic_index_in_dim(qpos, mine, 0, False)
    my_len = lax.dynamic_index_in_dim(prompt_len, mine, 0, False)
    my_qpos = jnp.where(my_qpos < my_len, my_qpos, -1)
    all_q = jnp.stack([q_mine, q_pair]).reshape(-1, HEAD_SIZE)
    all_qpos = jnp.broadcast_to(my_qpos[None, :, None], (2, span, heads_here)).reshape(-1, 1)
    context = attend(all_q, near, far, all_qpos, kpos).reshape(2, span, heads_here * HEAD_SIZE)
    c_mine = context[0]
    c_pair = swap_x(context[1])
    context = jnp.concatenate(
        [jnp.where(mine == 0, c_mine, c_pair), jnp.where(mine == 0, c_pair, c_mine)], axis=0
    )

    def partial(weight):
        weight = weight.reshape(rows_y, rows_z * piece, -1)
        return jnp.einsum("td,gnd->gtn", context, weight, preferred_element_type=jnp.float32)

    send = jnp.concatenate([partial(wo_near), partial(wo_far)], axis=2).astype(jnp.bfloat16)
    terms = lax.all_to_all(send, REP, split_axis=0, concat_axis=0, tiled=True)
    summed = jnp.sum(terms.astype(jnp.float32), axis=0).astype(jnp.bfloat16)
    summed = summed.reshape(2 * span, 2, rows_z, piece)
    first = jnp.where(core == 0, summed[:, 0], summed[:, 1])
    second = jnp.where(core == 0, summed[:, 1], summed[:, 0])
    attn_out = jnp.stack([first, second], axis=2).reshape(2, 1, 2, blk, -1)
    new_cache = settle_pages(cache_pages, move_page, arrived)
    return (attn_out, new_cache)


def solution(mesh):
    ctx, rep = mesh.devices.shape
    fine = Mesh(mesh.devices.reshape(rep, ctx // rep // 2, 2, 2, rep // 2), CTX + REP)
    return jax.shard_map(
        on_device,
        mesh=fine,
        in_specs=(
            P(None, CTX, None, None, None),
            P(),
            P(CTX, REP),
            P(CTX, None),
            P(CTX, None),
            P(REP, CTX),
            P(),
            P(),
            P(CTX, REP, None, None, None),
            P(CTX, REP, None),
            P(CTX, REP, None),
            P(CTX, REP, None),
        ),
        out_specs=(P(None, CTX, None, None, REP), P(CTX, REP, None, None, None)),
        check_vma=False,
    )
```

```python
import math

import jax
import jax.numpy as jnp
from jax import lax
from jax.experimental import pallas as pl
from jax.experimental.pallas import tpu as pltpu
from jax.sharding import Mesh
from jax.sharding import PartitionSpec as P

HEAD_SIZE = 128
HEADS_PER_KV = 8

CTX = ("y", "zh", "core")
REP = ("zl", "x")
CHIPS = ("y", "zh")

rope_base = 5000000.0
neg_fill = -1e30


def rope_tables(positions):
    half = HEAD_SIZE // 2
    steps_f = jnp.arange(half, dtype=jnp.float32) * (2.0 / HEAD_SIZE)
    freq = jnp.exp(-steps_f * math.log(rope_base))
    angle = positions.astype(jnp.float32)[:, None] * freq[None, :]
    return (jnp.cos(angle), jnp.sin(angle))


def apply_rotation(values, cosine_table, sine_table):
    half = values.shape[-1] // 2
    first = values[..., :half]
    second = values[..., half:]
    cosine_table = cosine_table[:, None, :]
    sine_table = sine_table[:, None, :]
    return jnp.concatenate(
        [first * cosine_table - second * sine_table, second * cosine_table + first * sine_table],
        axis=-1,
    )


def matmul(left, right):
    return jnp.dot(left, right, preferred_element_type=jnp.float32)


def spread(block, axes):
    size = lax.axis_size(axes)
    copies = jnp.broadcast_to(block[None], (size,) + block.shape)
    return lax.all_to_all(copies, axes, split_axis=0, concat_axis=0, tiled=True)


def swap_core(value):
    return lax.ppermute(value, "core", [(0, 1), (1, 0)])


def swap_x(value):
    return lax.ppermute(value, "x", [(i, i ^ 1) for i in range(lax.axis_size("x"))])


def norm_kernel(core_ref, hidden_ref, gain_ref, near_ref, far_ref):
    hidden = hidden_ref[...].astype(jnp.float32)
    scale = lax.rsqrt(jnp.mean(hidden * hidden, axis=-1, keepdims=True) + 1e-05)
    normed = hidden * scale * gain_ref[...].astype(jnp.float32)
    core = core_ref[0]
    lane = lax.broadcasted_iota(jnp.int32, (hidden.shape[0], 128), 1)
    for pair in range(hidden.shape[1] // 256):
        left = normed[:, 256 * pair : 256 * pair + 128]
        right = normed[:, 256 * pair + 128 : 256 * pair + 256]
        even = jnp.where(lane < 64, left, pltpu.roll(right, 64, 1)).astype(jnp.bfloat16)
        odd = jnp.where(lane < 64, pltpu.roll(left, 64, 1), right).astype(jnp.bfloat16)
        span = slice(128 * pair, 128 * pair + 128)
        near_ref[:, span] = jnp.where(core == 0, even, odd)
        far_ref[:, span] = jnp.where(core == 0, odd, even)


def split_norm(hidden, gain, core):
    rows, width = hidden.shape
    tile = 32
    half = jax.ShapeDtypeStruct((rows, width // 2), jnp.bfloat16)
    half_spec = pl.BlockSpec((tile, width // 2), lambda i: (i, 0))
    return pl.pallas_call(
        norm_kernel,
        grid=(rows // tile,),
        in_specs=[
            pl.BlockSpec(memory_space=pltpu.SMEM),
            pl.BlockSpec((tile, width), lambda i: (i, 0)),
            pl.BlockSpec((1, width), lambda i: (0, 0)),
        ],
        out_specs=(half_spec, half_spec),
        out_shape=(half, half),
        name="split_norm",
    )(core.reshape(1), hidden, gain[None])


def attend_kernel(q_ref, near_ref, far_ref, qpos_ref, kpos_ref, out_ref):
    half = near_ref.shape[0]
    queries = q_ref[...]
    scores = []
    masks = []
    for part, ref in enumerate((near_ref, far_ref)):
        keys = ref[:, :HEAD_SIZE]
        raw = lax.dot_general(
            queries, keys, (((1,), (1,)), ((), ())), preferred_element_type=jnp.float32
        )
        raw = raw * HEAD_SIZE ** (-0.5)
        allowed = kpos_ref[:, part * half : (part + 1) * half] <= qpos_ref[...]
        scores.append(raw)
        masks.append(allowed)
    top = jnp.maximum(
        jnp.max(jnp.where(masks[0], scores[0], neg_fill), axis=-1, keepdims=True),
        jnp.max(jnp.where(masks[1], scores[1], neg_fill), axis=-1, keepdims=True),
    )
    total = jnp.zeros_like(top)
    acc = jnp.zeros(out_ref.shape, jnp.float32)
    for raw, allowed, ref in zip(scores, masks, (near_ref, far_ref)):
        weights = jnp.where(allowed, jnp.exp(raw - top), 0.0)
        total = total + jnp.sum(weights, axis=-1, keepdims=True)
        acc = acc + matmul(weights.astype(jnp.bfloat16), ref[:, HEAD_SIZE:])
    out_ref[...] = (acc / jnp.maximum(total, 1.0)).astype(jnp.bfloat16)


def attend(queries, near, far, qpos, kpos):
    rows, half = queries.shape[0], near.shape[0]
    tile = min(rows, 128)
    return pl.pallas_call(
        attend_kernel,
        grid=(rows // tile,),
        in_specs=[
            pl.BlockSpec((tile, HEAD_SIZE), lambda i: (i, 0)),
            pl.BlockSpec((half, 2 * HEAD_SIZE), lambda i: (0, 0)),
            pl.BlockSpec((half, 2 * HEAD_SIZE), lambda i: (0, 0)),
            pl.BlockSpec((tile, 1), lambda i: (i, 0)),
            pl.BlockSpec((1, 2 * half), lambda i: (0, 0)),
        ],
        out_specs=pl.BlockSpec((tile, HEAD_SIZE), lambda i: (i, 0)),
        out_shape=jax.ShapeDtypeStruct((rows, HEAD_SIZE), jnp.bfloat16),
        compiler_params=pltpu.CompilerParams(vmem_limit_bytes=40 << 20),
        name="attend",
    )(queries, near, far, qpos, kpos)


def pages_to_send(cache_pages, move_page, move_dest, move_slot):
    pages = cache_pages[0, 0]
    page_count = pages.shape[0]
    moves = move_page.shape[2]
    groups = lax.axis_size(REP)
    leave_ids = move_page[0, 0]
    dest_ids = move_dest[0, 0]
    slot_ids = move_slot[0, 0] - (page_count - moves)
    slots = jnp.arange(moves, dtype=jnp.int32)
    leaving = jnp.take(pages, leave_ids, axis=0)
    to_dest = dest_ids[None, :] == jnp.arange(groups, dtype=jnp.int32)[:, None]
    chosen = to_dest[:, None, :] & (slot_ids[None, :] == slots[:, None])[None]
    send = jnp.zeros((groups, moves) + pages.shape[1:], pages.dtype)
    for move in range(moves):
        send = jnp.where(chosen[:, :, move, None, None], leaving[move][None, None], send)
    return send


def settle_pages(cache_pages, move_page, arrived):
    pages = cache_pages[0, 0]
    page_count = pages.shape[0]
    moves = move_page.shape[2]
    leave_ids = move_page[0, 0]
    gone = jnp.any(leave_ids[:, None] == jnp.arange(page_count, dtype=jnp.int32)[None, :], axis=0)
    kept = jnp.where(gone[:, None, None], jnp.zeros_like(pages), pages)
    new_pages = jnp.concatenate([kept[: page_count - moves], arrived[0]], axis=0)
    return new_pages.reshape(cache_pages.shape)


def on_device(
    hidden_in,
    norm_gain,
    w_query,
    key_matrix,
    value_matrix,
    w_out,
    prompt_len,
    pair_of_device,
    cache_pages,
    move_page,
    move_dest,
    move_slot,
):
    cycle = lax.axis_size(CTX)
    place = lax.axis_index(CTX)
    rank = lax.axis_index(REP)
    core = lax.axis_index("core")
    rows_y, rows_z = lax.axis_size("y"), lax.axis_size("zh")
    mine = lax.axis_index("x") % 2
    blk = hidden_in.shape[3]
    span = 2 * blk
    width = hidden_in.shape[4]
    piece = w_query.shape[0]
    heads_here = w_query.shape[1] // HEAD_SIZE
    kv_first = (rank * heads_here // HEADS_PER_KV) * HEAD_SIZE

    key_cols = lax.dynamic_slice_in_dim(key_matrix, kv_first, HEAD_SIZE, 1)
    value_cols = lax.dynamic_slice_in_dim(value_matrix, kv_first, HEAD_SIZE, 1)
    half_near = spread(jnp.where(mine == 0, key_cols, value_cols), CHIPS).reshape(-1, HEAD_SIZE)
    weights = jnp.stack([w_query, w_out.T])
    weights = lax.all_gather(weights, "zh", axis=0)
    weights, leave = lax.optimization_barrier((weights, move_page))
    weights = lax.all_gather(weights, "y", axis=0)
    send_pages = pages_to_send(cache_pages, leave, move_dest, move_slot)
    arrived = lax.psum_scatter(send_pages, REP, scatter_dimension=0, tiled=True)
    weights, arrived = lax.optimization_barrier((weights, arrived))
    wq_near = weights[:, :, 0].reshape(rows_y * rows_z * piece, -1)
    wo_near = weights[:, :, 1].reshape(rows_y * rows_z * piece, -1)
    wq_far = swap_core(wq_near)

    x_near, x_far = split_norm(hidden_in.reshape(2 * span, width), norm_gain, core)
    half_near, x_near, x_far = lax.optimization_barrier((half_near, x_near, x_far))
    half_far = swap_core(half_near)

    own_pair = lax.dynamic_slice_in_dim(pair_of_device, place, 1, 1)[:, 0]
    blocks = jnp.stack([own_pair, 2 * cycle - 1 - own_pair], axis=1)
    qpos = (blocks[:, :, None] * blk + jnp.arange(blk, dtype=jnp.int32)).reshape(2, span)
    cosine_table, sine_table = rope_tables(qpos.reshape(-1))

    half = matmul(x_near, half_near) + matmul(x_far, half_far)
    keys = apply_rotation(half[:, None, :], cosine_table, sine_table)[:, 0]
    half = jnp.where(mine == 0, keys, half).astype(jnp.bfloat16).reshape(2, span, HEAD_SIZE)
    kept = lax.dynamic_index_in_dim(half, mine, 0, False)
    other = swap_x(lax.dynamic_index_in_dim(half, 1 - mine, 0, False))
    kv = jnp.where(
        mine == 0,
        jnp.concatenate([kept, other], axis=1),
        jnp.concatenate([other, kept], axis=1),
    )
    near = spread(kv, CHIPS).reshape(-1, 2 * HEAD_SIZE)
    far = swap_core(near)

    query = matmul(x_near, wq_near) + matmul(x_far, wq_far)
    query = apply_rotation(
        query.reshape(2 * span, heads_here, HEAD_SIZE), cosine_table, sine_table
    ).astype(jnp.bfloat16)
    query = query.reshape(2, span, heads_here * HEAD_SIZE)
    q_mine = lax.dynamic_index_in_dim(query, mine, 0, False)
    q_pair = swap_x(lax.dynamic_index_in_dim(query, 1 - mine, 0, False))

    wo_far = swap_core(wo_near)

    pairs = lax.dynamic_index_in_dim(pair_of_device, mine, 0, False).reshape(-1, 2)
    pairs = jnp.where(core == 0, pairs, pairs[:, ::-1]).T.reshape(-1)
    kblocks = jnp.stack([pairs, 2 * cycle - 1 - pairs], axis=1)
    kpos = (kblocks[..., None] * blk + jnp.arange(blk, dtype=jnp.int32)).reshape(1, -1)
    my_qpos = lax.dynamic_index_in_dim(qpos, mine, 0, False)
    my_len = lax.dynamic_index_in_dim(prompt_len, mine, 0, False)
    my_qpos = jnp.where(my_qpos < my_len, my_qpos, -1)
    all_q = jnp.stack([q_mine, q_pair]).reshape(-1, HEAD_SIZE)
    all_qpos = jnp.broadcast_to(my_qpos[None, :, None], (2, span, heads_here)).reshape(-1, 1)
    context = attend(all_q, near, far, all_qpos, kpos).reshape(2, span, heads_here * HEAD_SIZE)
    c_mine = context[0]
    c_pair = swap_x(context[1])
    context = jnp.concatenate(
        [jnp.where(mine == 0, c_mine, c_pair), jnp.where(mine == 0, c_pair, c_mine)], axis=0
    )

    def partial(weight):
        weight = weight.reshape(rows_y, rows_z * piece, -1)
        return jnp.einsum("td,gnd->gtn", context, weight, preferred_element_type=jnp.float32)

    send = jnp.concatenate([partial(wo_near), partial(wo_far)], axis=2).astype(jnp.bfloat16)
    terms = lax.all_to_all(send, REP, split_axis=0, concat_axis=0, tiled=True)
    summed = jnp.sum(terms.astype(jnp.float32), axis=0).astype(jnp.bfloat16)
    summed = summed.reshape(2 * span, 2, rows_z, piece)
    first = jnp.where(core == 0, summed[:, 0], summed[:, 1])
    second = jnp.where(core == 0, summed[:, 1], summed[:, 0])
    attn_out = jnp.stack([first, second], axis=2).reshape(2, 1, 2, blk, -1)
    new_cache = settle_pages(cache_pages, move_page, arrived)
    return (attn_out, new_cache)


def solution(mesh):
    ctx, rep = mesh.devices.shape
    fine = Mesh(mesh.devices.reshape(rep, ctx // rep // 2, 2, 2, rep // 2), CTX + REP)
    return jax.shard_map(
        on_device,
        mesh=fine,
        in_specs=(
            P(None, CTX, None, None, None),
            P(),
            P(CTX, REP),
            P(CTX, None),
            P(CTX, None),
            P(REP, CTX),
            P(),
            P(),
            P(CTX, REP, None, None, None),
            P(CTX, REP, None),
            P(CTX, REP, None),
            P(CTX, REP, None),
        ),
        out_specs=(P(None, CTX, None, None, REP), P(CTX, REP, None, None, None)),
        check_vma=False,
    )
```

```python
import math

import jax
import jax.numpy as jnp
from jax import lax
from jax.experimental import pallas as pl
from jax.experimental.pallas import tpu as pltpu
from jax.sharding import Mesh
from jax.sharding import PartitionSpec as P

HEAD_SIZE = 128
HEADS_PER_KV = 8

CTX = ("y", "zh", "core")
REP = ("zl", "x")
CHIPS = ("y", "zh")

rope_base = 5000000.0
neg_fill = -1e30


def rope_tables(positions):
    half = HEAD_SIZE // 2
    steps_f = jnp.arange(half, dtype=jnp.float32) * (2.0 / HEAD_SIZE)
    freq = jnp.exp(-steps_f * math.log(rope_base))
    angle = positions.astype(jnp.float32)[:, None] * freq[None, :]
    return (jnp.cos(angle), jnp.sin(angle))


def apply_rotation(values, cosine_table, sine_table):
    half = values.shape[-1] // 2
    first = values[..., :half]
    second = values[..., half:]
    cosine_table = cosine_table[:, None, :]
    sine_table = sine_table[:, None, :]
    return jnp.concatenate(
        [first * cosine_table - second * sine_table, second * cosine_table + first * sine_table],
        axis=-1,
    )


def matmul(left, right):
    return jnp.dot(left, right, preferred_element_type=jnp.float32)


def spread(block, axes):
    size = lax.axis_size(axes)
    copies = jnp.broadcast_to(block[None], (size,) + block.shape)
    return lax.all_to_all(copies, axes, split_axis=0, concat_axis=0, tiled=True)


def swap_core(value):
    return lax.ppermute(value, "core", [(0, 1), (1, 0)])


def swap_x(value):
    return lax.ppermute(value, "x", [(i, i ^ 1) for i in range(lax.axis_size("x"))])


def norm_kernel(core_ref, hidden_ref, gain_ref, near_ref, far_ref):
    hidden = hidden_ref[...].astype(jnp.float32)
    scale = lax.rsqrt(jnp.mean(hidden * hidden, axis=-1, keepdims=True) + 1e-05)
    normed = hidden * scale * gain_ref[...].astype(jnp.float32)
    core = core_ref[0]
    lane = lax.broadcasted_iota(jnp.int32, (hidden.shape[0], 128), 1)
    for pair in range(hidden.shape[1] // 256):
        left = normed[:, 256 * pair : 256 * pair + 128]
        right = normed[:, 256 * pair + 128 : 256 * pair + 256]
        even = jnp.where(lane < 64, left, pltpu.roll(right, 64, 1)).astype(jnp.bfloat16)
        odd = jnp.where(lane < 64, pltpu.roll(left, 64, 1), right).astype(jnp.bfloat16)
        span = slice(128 * pair, 128 * pair + 128)
        near_ref[:, span] = jnp.where(core == 0, even, odd)
        far_ref[:, span] = jnp.where(core == 0, odd, even)


def split_norm(hidden, gain, core):
    rows, width = hidden.shape
    tile = 32
    half = jax.ShapeDtypeStruct((rows, width // 2), jnp.bfloat16)
    half_spec = pl.BlockSpec((tile, width // 2), lambda i: (i, 0))
    return pl.pallas_call(
        norm_kernel,
        grid=(rows // tile,),
        in_specs=[
            pl.BlockSpec(memory_space=pltpu.SMEM),
            pl.BlockSpec((tile, width), lambda i: (i, 0)),
            pl.BlockSpec((1, width), lambda i: (0, 0)),
        ],
        out_specs=(half_spec, half_spec),
        out_shape=(half, half),
        name="split_norm",
    )(core.reshape(1), hidden, gain[None])


def attend_kernel(q_ref, near_ref, far_ref, qpos_ref, kpos_ref, out_ref):
    half = near_ref.shape[0]
    queries = q_ref[...]
    scores = []
    masks = []
    for part, ref in enumerate((near_ref, far_ref)):
        keys = ref[:, :HEAD_SIZE]
        raw = lax.dot_general(
            queries, keys, (((1,), (1,)), ((), ())), preferred_element_type=jnp.float32
        )
        raw = raw * HEAD_SIZE ** (-0.5)
        allowed = kpos_ref[:, part * half : (part + 1) * half] <= qpos_ref[...]
        scores.append(raw)
        masks.append(allowed)
    top = jnp.maximum(
        jnp.max(jnp.where(masks[0], scores[0], neg_fill), axis=-1, keepdims=True),
        jnp.max(jnp.where(masks[1], scores[1], neg_fill), axis=-1, keepdims=True),
    )
    total = jnp.zeros_like(top)
    acc = jnp.zeros(out_ref.shape, jnp.float32)
    for raw, allowed, ref in zip(scores, masks, (near_ref, far_ref)):
        weights = jnp.where(allowed, jnp.exp(raw - top), 0.0)
        total = total + jnp.sum(weights, axis=-1, keepdims=True)
        acc = acc + matmul(weights.astype(jnp.bfloat16), ref[:, HEAD_SIZE:])
    out_ref[...] = (acc / jnp.maximum(total, 1.0)).astype(jnp.bfloat16)


def attend(queries, near, far, qpos, kpos):
    rows, half = queries.shape[0], near.shape[0]
    tile = min(rows, 128)
    return pl.pallas_call(
        attend_kernel,
        grid=(rows // tile,),
        in_specs=[
            pl.BlockSpec((tile, HEAD_SIZE), lambda i: (i, 0)),
            pl.BlockSpec((half, 2 * HEAD_SIZE), lambda i: (0, 0)),
            pl.BlockSpec((half, 2 * HEAD_SIZE), lambda i: (0, 0)),
            pl.BlockSpec((tile, 1), lambda i: (i, 0)),
            pl.BlockSpec((1, 2 * half), lambda i: (0, 0)),
        ],
        out_specs=pl.BlockSpec((tile, HEAD_SIZE), lambda i: (i, 0)),
        out_shape=jax.ShapeDtypeStruct((rows, HEAD_SIZE), jnp.bfloat16),
        compiler_params=pltpu.CompilerParams(vmem_limit_bytes=40 << 20),
        name="attend",
    )(queries, near, far, qpos, kpos)


def pages_kernel(page_ref, dest_ref, slot_ref, cache_ref, send_ref):
    groups, moves = send_ref.shape[:2]
    free = cache_ref.shape[0] - moves
    leaving = [cache_ref[page_ref[move]] for move in range(moves)]
    for group in range(groups):
        for slot in range(moves):
            page = jnp.zeros_like(leaving[0])
            for move in range(moves):
                here = (dest_ref[move] == group) & (slot_ref[move] == free + slot)
                page = jnp.where(here, leaving[move], page)
            send_ref[group, slot] = page


def pages_to_send(cache_pages, move_page, move_dest, move_slot):
    pages = cache_pages[0, 0]
    shape = (lax.axis_size(REP), move_page.shape[2]) + pages.shape[1:]
    scalars = pl.BlockSpec(memory_space=pltpu.SMEM)
    vector = pl.BlockSpec(memory_space=pltpu.VMEM)
    return pl.pallas_call(
        pages_kernel,
        in_specs=[scalars, scalars, scalars, vector],
        out_specs=vector,
        out_shape=jax.ShapeDtypeStruct(shape, pages.dtype),
        name="pages_to_send",
    )(move_page[0, 0], move_dest[0, 0], move_slot[0, 0], pages)


def settle_pages(cache_pages, move_page, arrived):
    pages = cache_pages[0, 0]
    page_count = pages.shape[0]
    moves = move_page.shape[2]
    leave_ids = move_page[0, 0]
    gone = jnp.any(leave_ids[:, None] == jnp.arange(page_count, dtype=jnp.int32)[None, :], axis=0)
    kept = jnp.where(gone[:, None, None], jnp.zeros_like(pages), pages)
    new_pages = jnp.concatenate([kept[: page_count - moves], arrived[0]], axis=0)
    return new_pages.reshape(cache_pages.shape)


def on_device(
    hidden_in,
    norm_gain,
    w_query,
    key_matrix,
    value_matrix,
    w_out,
    prompt_len,
    pair_of_device,
    cache_pages,
    move_page,
    move_dest,
    move_slot,
):
    cycle = lax.axis_size(CTX)
    place = lax.axis_index(CTX)
    rank = lax.axis_index(REP)
    core = lax.axis_index("core")
    rows_y, rows_z = lax.axis_size("y"), lax.axis_size("zh")
    mine = lax.axis_index("x") % 2
    blk = hidden_in.shape[3]
    span = 2 * blk
    width = hidden_in.shape[4]
    piece = w_query.shape[0]
    heads_here = w_query.shape[1] // HEAD_SIZE
    kv_first = (rank * heads_here // HEADS_PER_KV) * HEAD_SIZE

    key_cols = lax.dynamic_slice_in_dim(key_matrix, kv_first, HEAD_SIZE, 1)
    value_cols = lax.dynamic_slice_in_dim(value_matrix, kv_first, HEAD_SIZE, 1)
    half_near = spread(jnp.where(mine == 0, key_cols, value_cols), CHIPS).reshape(-1, HEAD_SIZE)
    weights = lax.all_gather(jnp.stack([w_query, w_out.T]), "zh", axis=0)
    weights, leave = lax.optimization_barrier((weights, move_page))
    wq_near = weights[:, 0].reshape(rows_z * piece, -1)
    wo_near = weights[:, 1].reshape(rows_z * piece, -1)
    wq_near = lax.all_gather(wq_near, "y", axis=0, tiled=True)

    x_near, x_far = split_norm(hidden_in.reshape(2 * span, width), norm_gain, core)
    send_pages = pages_to_send(cache_pages, leave, move_dest, move_slot)
    arrived = lax.psum_scatter(send_pages, REP, scatter_dimension=0, tiled=True)
    half_near, x_near, x_far, wo_near = lax.optimization_barrier(
        (half_near, x_near, x_far, wo_near)
    )
    wo_near = lax.all_gather(wo_near, "y", axis=0, tiled=True)
    half_far = swap_core(half_near)
    x_chip = jnp.concatenate([x_near, swap_core(x_far)], axis=0)

    own_pair = lax.dynamic_slice_in_dim(pair_of_device, place, 1, 1)[:, 0]
    blocks = jnp.stack([own_pair, 2 * cycle - 1 - own_pair], axis=1)
    qpos = (blocks[:, :, None] * blk + jnp.arange(blk, dtype=jnp.int32)).reshape(2, span)
    cosine_table, sine_table = rope_tables(qpos.reshape(-1))

    half = matmul(x_near, half_near) + matmul(x_far, half_far)
    keys = apply_rotation(half[:, None, :], cosine_table, sine_table)[:, 0]
    half = jnp.where(mine == 0, keys, half).astype(jnp.bfloat16).reshape(2, span, HEAD_SIZE)
    kept = lax.dynamic_index_in_dim(half, mine, 0, False)
    other = swap_x(lax.dynamic_index_in_dim(half, 1 - mine, 0, False))
    kv = jnp.where(
        mine == 0,
        jnp.concatenate([kept, other], axis=1),
        jnp.concatenate([other, kept], axis=1),
    )
    kv, x_chip = lax.optimization_barrier((kv, x_chip))
    near = spread(kv, CHIPS).reshape(-1, 2 * HEAD_SIZE)
    wq_near, arrived = lax.optimization_barrier((wq_near, arrived))
    query = matmul(x_chip, wq_near)
    query = query[: 2 * span] + swap_core(query[2 * span :])
    query = apply_rotation(
        query.reshape(2 * span, heads_here, HEAD_SIZE), cosine_table, sine_table
    ).astype(jnp.bfloat16)
    query = query.reshape(2, span, heads_here * HEAD_SIZE)
    q_mine = lax.dynamic_index_in_dim(query, mine, 0, False)
    q_pair = swap_x(lax.dynamic_index_in_dim(query, 1 - mine, 0, False))

    pairs = lax.dynamic_index_in_dim(pair_of_device, mine, 0, False).reshape(-1, 2)
    pairs = jnp.where(core == 0, pairs, pairs[:, ::-1]).T.reshape(-1)
    kblocks = jnp.stack([pairs, 2 * cycle - 1 - pairs], axis=1)
    kpos = (kblocks[..., None] * blk + jnp.arange(blk, dtype=jnp.int32)).reshape(1, -1)
    my_qpos = lax.dynamic_index_in_dim(qpos, mine, 0, False)
    my_len = lax.dynamic_index_in_dim(prompt_len, mine, 0, False)
    my_qpos = jnp.where(my_qpos < my_len, my_qpos, -1)
    all_q = jnp.stack([q_mine, q_pair]).reshape(-1, HEAD_SIZE)
    near, all_q = lax.optimization_barrier((near, all_q))
    far = swap_core(near)
    all_qpos = jnp.broadcast_to(my_qpos[None, :, None], (2, span, heads_here)).reshape(-1, 1)
    context = attend(all_q, near, far, all_qpos, kpos).reshape(2, span, heads_here * HEAD_SIZE)
    c_pair = swap_x(context[1])
    wo_near, c_pair = lax.optimization_barrier((wo_near, c_pair))
    c_mine = context[0]
    wo_far = swap_core(wo_near)
    context = jnp.concatenate(
        [jnp.where(mine == 0, c_mine, c_pair), jnp.where(mine == 0, c_pair, c_mine)], axis=0
    )

    def partial(weight):
        weight = weight.reshape(rows_y, rows_z * piece, -1)
        return jnp.einsum("td,gnd->gtn", context, weight, preferred_element_type=jnp.float32)

    send = jnp.concatenate([partial(wo_near), partial(wo_far)], axis=2).astype(jnp.bfloat16)
    terms = lax.all_to_all(send, REP, split_axis=0, concat_axis=0, tiled=True)
    summed = jnp.sum(terms.astype(jnp.float32), axis=0).astype(jnp.bfloat16)
    summed = summed.reshape(2 * span, 2, rows_z, piece)
    first = jnp.where(core == 0, summed[:, 0], summed[:, 1])
    second = jnp.where(core == 0, summed[:, 1], summed[:, 0])
    attn_out = jnp.stack([first, second], axis=2).reshape(2, 1, 2, blk, -1)
    new_cache = settle_pages(cache_pages, move_page, arrived)
    return (attn_out, new_cache)


def solution(mesh):
    ctx, rep = mesh.devices.shape
    fine = Mesh(mesh.devices.reshape(rep, ctx // rep // 2, 2, 2, rep // 2), CTX + REP)
    return jax.shard_map(
        on_device,
        mesh=fine,
        in_specs=(
            P(None, CTX, None, None, None),
            P(),
            P(CTX, REP),
            P(CTX, None),
            P(CTX, None),
            P(REP, CTX),
            P(),
            P(),
            P(CTX, REP, None, None, None),
            P(CTX, REP, None),
            P(CTX, REP, None),
            P(CTX, REP, None),
        ),
        out_specs=(P(None, CTX, None, None, REP), P(CTX, REP, None, None, None)),
        check_vma=False,
    )
```

```python
import math

import jax
import jax.numpy as jnp
from jax import lax
from jax.experimental import pallas as pl
from jax.experimental.pallas import tpu as pltpu
from jax.sharding import Mesh
from jax.sharding import PartitionSpec as P

HEAD_SIZE = 128
HEADS_PER_KV = 8

CTX = ("y", "zh", "core")
REP = ("zl", "x")
CHIPS = ("y", "zh")

rope_base = 5000000.0
neg_fill = -1e30


def rope_tables(positions):
    half = HEAD_SIZE // 2
    steps_f = jnp.arange(half, dtype=jnp.float32) * (2.0 / HEAD_SIZE)
    freq = jnp.exp(-steps_f * math.log(rope_base))
    angle = positions.astype(jnp.float32)[:, None] * freq[None, :]
    return (jnp.cos(angle), jnp.sin(angle))


def apply_rotation(values, cosine_table, sine_table):
    half = values.shape[-1] // 2
    first = values[..., :half]
    second = values[..., half:]
    cosine_table = cosine_table[:, None, :]
    sine_table = sine_table[:, None, :]
    return jnp.concatenate(
        [first * cosine_table - second * sine_table, second * cosine_table + first * sine_table],
        axis=-1,
    )


def matmul(left, right):
    return jnp.dot(left, right, preferred_element_type=jnp.float32)


def spread(block, axes):
    size = lax.axis_size(axes)
    copies = jnp.broadcast_to(block[None], (size,) + block.shape)
    return lax.all_to_all(copies, axes, split_axis=0, concat_axis=0, tiled=True)


def swap_core(value):
    return lax.ppermute(value, "core", [(0, 1), (1, 0)])


def swap_x(value):
    return lax.ppermute(value, "x", [(i, i ^ 1) for i in range(lax.axis_size("x"))])


def norm_kernel(core_ref, hidden_ref, gain_ref, near_ref, far_ref):
    hidden = hidden_ref[...].astype(jnp.float32)
    scale = lax.rsqrt(jnp.mean(hidden * hidden, axis=-1, keepdims=True) + 1e-05)
    normed = hidden * scale * gain_ref[...].astype(jnp.float32)
    core = core_ref[0]
    lane = lax.broadcasted_iota(jnp.int32, (hidden.shape[0], 128), 1)
    for pair in range(hidden.shape[1] // 256):
        left = normed[:, 256 * pair : 256 * pair + 128]
        right = normed[:, 256 * pair + 128 : 256 * pair + 256]
        even = jnp.where(lane < 64, left, pltpu.roll(right, 64, 1)).astype(jnp.bfloat16)
        odd = jnp.where(lane < 64, pltpu.roll(left, 64, 1), right).astype(jnp.bfloat16)
        span = slice(128 * pair, 128 * pair + 128)
        near_ref[:, span] = jnp.where(core == 0, even, odd)
        far_ref[:, span] = jnp.where(core == 0, odd, even)


def split_norm(hidden, gain, core):
    rows, width = hidden.shape
    tile = 32
    half = jax.ShapeDtypeStruct((rows, width // 2), jnp.bfloat16)
    half_spec = pl.BlockSpec((tile, width // 2), lambda i: (i, 0))
    return pl.pallas_call(
        norm_kernel,
        grid=(rows // tile,),
        in_specs=[
            pl.BlockSpec(memory_space=pltpu.SMEM),
            pl.BlockSpec((tile, width), lambda i: (i, 0)),
            pl.BlockSpec((1, width), lambda i: (0, 0)),
        ],
        out_specs=(half_spec, half_spec),
        out_shape=(half, half),
        name="split_norm",
    )(core.reshape(1), hidden, gain[None])


def attend_kernel(q_ref, near_ref, far_ref, qpos_ref, kpos_ref, out_ref):
    half = near_ref.shape[0]
    queries = q_ref[...]
    scores = []
    masks = []
    for part, ref in enumerate((near_ref, far_ref)):
        keys = ref[:, :HEAD_SIZE]
        raw = lax.dot_general(
            queries, keys, (((1,), (1,)), ((), ())), preferred_element_type=jnp.float32
        )
        raw = raw * HEAD_SIZE ** (-0.5)
        allowed = kpos_ref[:, part * half : (part + 1) * half] <= qpos_ref[...]
        scores.append(raw)
        masks.append(allowed)
    top = jnp.maximum(
        jnp.max(jnp.where(masks[0], scores[0], neg_fill), axis=-1, keepdims=True),
        jnp.max(jnp.where(masks[1], scores[1], neg_fill), axis=-1, keepdims=True),
    )
    total = jnp.zeros_like(top)
    acc = jnp.zeros(out_ref.shape, jnp.float32)
    for raw, allowed, ref in zip(scores, masks, (near_ref, far_ref)):
        weights = jnp.where(allowed, jnp.exp(raw - top), 0.0)
        total = total + jnp.sum(weights, axis=-1, keepdims=True)
        acc = acc + matmul(weights.astype(jnp.bfloat16), ref[:, HEAD_SIZE:])
    out_ref[...] = (acc / jnp.maximum(total, 1.0)).astype(jnp.bfloat16)


def attend(queries, near, far, qpos, kpos):
    rows, half = queries.shape[0], near.shape[0]
    tile = min(rows, 128)
    return pl.pallas_call(
        attend_kernel,
        grid=(rows // tile,),
        in_specs=[
            pl.BlockSpec((tile, HEAD_SIZE), lambda i: (i, 0)),
            pl.BlockSpec((half, 2 * HEAD_SIZE), lambda i: (0, 0)),
            pl.BlockSpec((half, 2 * HEAD_SIZE), lambda i: (0, 0)),
            pl.BlockSpec((tile, 1), lambda i: (i, 0)),
            pl.BlockSpec((1, 2 * half), lambda i: (0, 0)),
        ],
        out_specs=pl.BlockSpec((tile, HEAD_SIZE), lambda i: (i, 0)),
        out_shape=jax.ShapeDtypeStruct((rows, HEAD_SIZE), jnp.bfloat16),
        compiler_params=pltpu.CompilerParams(vmem_limit_bytes=40 << 20),
        name="attend",
    )(queries, near, far, qpos, kpos)


def pages_kernel(page_ref, dest_ref, slot_ref, cache_ref, send_ref):
    groups, moves = send_ref.shape[:2]
    free = cache_ref.shape[0] - moves
    leaving = [cache_ref[page_ref[move]] for move in range(moves)]
    for group in range(groups):
        for slot in range(moves):
            page = jnp.zeros_like(leaving[0])
            for move in range(moves):
                here = (dest_ref[move] == group) & (slot_ref[move] == free + slot)
                page = jnp.where(here, leaving[move], page)
            send_ref[group, slot] = page


def pages_to_send(cache_pages, move_page, move_dest, move_slot):
    pages = cache_pages[0, 0]
    shape = (lax.axis_size(REP), move_page.shape[2]) + pages.shape[1:]
    scalars = pl.BlockSpec(memory_space=pltpu.SMEM)
    vector = pl.BlockSpec(memory_space=pltpu.VMEM)
    return pl.pallas_call(
        pages_kernel,
        in_specs=[scalars, scalars, scalars, vector],
        out_specs=vector,
        out_shape=jax.ShapeDtypeStruct(shape, pages.dtype),
        name="pages_to_send",
    )(move_page[0, 0], move_dest[0, 0], move_slot[0, 0], pages)


def settle_pages(cache_pages, move_page, arrived):
    pages = cache_pages[0, 0]
    page_count = pages.shape[0]
    moves = move_page.shape[2]
    leave_ids = move_page[0, 0]
    gone = jnp.any(leave_ids[:, None] == jnp.arange(page_count, dtype=jnp.int32)[None, :], axis=0)
    kept = jnp.where(gone[:, None, None], jnp.zeros_like(pages), pages)
    new_pages = jnp.concatenate([kept[: page_count - moves], arrived[0]], axis=0)
    return new_pages.reshape(cache_pages.shape)


def on_device(
    hidden_in,
    norm_gain,
    w_query,
    key_matrix,
    value_matrix,
    w_out,
    prompt_len,
    pair_of_device,
    cache_pages,
    move_page,
    move_dest,
    move_slot,
):
    cycle = lax.axis_size(CTX)
    place = lax.axis_index(CTX)
    rank = lax.axis_index(REP)
    core = lax.axis_index("core")
    rows_y, rows_z = lax.axis_size("y"), lax.axis_size("zh")
    mine = lax.axis_index("x") % 2
    blk = hidden_in.shape[3]
    span = 2 * blk
    width = hidden_in.shape[4]
    piece = w_query.shape[0]
    heads_here = w_query.shape[1] // HEAD_SIZE
    kv_first = (rank * heads_here // HEADS_PER_KV) * HEAD_SIZE

    key_cols = lax.dynamic_slice_in_dim(key_matrix, kv_first, HEAD_SIZE, 1)
    value_cols = lax.dynamic_slice_in_dim(value_matrix, kv_first, HEAD_SIZE, 1)
    half_near = jnp.where(mine == 0, key_cols, value_cols)
    weights = jnp.concatenate([w_query, w_out.T, half_near], axis=1)
    weights = lax.all_gather(weights, "zh", axis=0, tiled=True)
    weights, leave = lax.optimization_barrier((weights, move_page))
    cols = w_query.shape[1]
    wq_near, wo_near = weights[:, :cols], weights[:, cols : 2 * cols]
    half_near = spread(weights[:, 2 * cols :], "y").reshape(-1, HEAD_SIZE)
    wq_near = lax.all_gather(wq_near, "y", axis=0, tiled=True)

    x_near, x_far = split_norm(hidden_in.reshape(2 * span, width), norm_gain, core)
    send_pages = pages_to_send(cache_pages, leave, move_dest, move_slot)
    arrived = lax.psum_scatter(send_pages, REP, scatter_dimension=0, tiled=True)
    x_other = swap_core(x_far)
    half_near, x_near, x_far, wo_near = lax.optimization_barrier(
        (half_near, x_near, x_far, wo_near)
    )
    wo_near = lax.all_gather(wo_near, "y", axis=0, tiled=True)
    half_far = swap_core(half_near)
    x_chip = jnp.concatenate([x_near, x_other], axis=0)

    own_pair = lax.dynamic_slice_in_dim(pair_of_device, place, 1, 1)[:, 0]
    blocks = jnp.stack([own_pair, 2 * cycle - 1 - own_pair], axis=1)
    qpos = (blocks[:, :, None] * blk + jnp.arange(blk, dtype=jnp.int32)).reshape(2, span)
    cosine_table, sine_table = rope_tables(qpos.reshape(-1))

    half = matmul(x_near, half_near) + matmul(x_far, half_far)
    keys = apply_rotation(half[:, None, :], cosine_table, sine_table)[:, 0]
    half = jnp.where(mine == 0, keys, half).astype(jnp.bfloat16).reshape(2, span, HEAD_SIZE)
    kept = lax.dynamic_index_in_dim(half, mine, 0, False)
    other = swap_x(lax.dynamic_index_in_dim(half, 1 - mine, 0, False))
    kv = jnp.where(
        mine == 0,
        jnp.concatenate([kept, other], axis=1),
        jnp.concatenate([other, kept], axis=1),
    )
    kv, x_chip = lax.optimization_barrier((kv, x_chip))
    near = spread(kv, CHIPS).reshape(-1, 2 * HEAD_SIZE)
    wq_near, arrived = lax.optimization_barrier((wq_near, arrived))
    query = matmul(x_chip, wq_near)
    query = query[: 2 * span] + swap_core(query[2 * span :])
    query = apply_rotation(
        query.reshape(2 * span, heads_here, HEAD_SIZE), cosine_table, sine_table
    ).astype(jnp.bfloat16)
    query = query.reshape(2, span, heads_here * HEAD_SIZE)
    q_mine = lax.dynamic_index_in_dim(query, mine, 0, False)
    q_pair = swap_x(lax.dynamic_index_in_dim(query, 1 - mine, 0, False))

    pairs = lax.dynamic_index_in_dim(pair_of_device, mine, 0, False).reshape(-1, 2)
    pairs = jnp.where(core == 0, pairs, pairs[:, ::-1]).T.reshape(-1)
    kblocks = jnp.stack([pairs, 2 * cycle - 1 - pairs], axis=1)
    kpos = (kblocks[..., None] * blk + jnp.arange(blk, dtype=jnp.int32)).reshape(1, -1)
    my_qpos = lax.dynamic_index_in_dim(qpos, mine, 0, False)
    my_len = lax.dynamic_index_in_dim(prompt_len, mine, 0, False)
    my_qpos = jnp.where(my_qpos < my_len, my_qpos, -1)
    all_q = jnp.stack([q_mine, q_pair]).reshape(-1, HEAD_SIZE)
    near, all_q = lax.optimization_barrier((near, all_q))
    far = swap_core(near)
    all_qpos = jnp.broadcast_to(my_qpos[None, :, None], (2, span, heads_here)).reshape(-1, 1)
    context = attend(all_q, near, far, all_qpos, kpos).reshape(2, span, heads_here * HEAD_SIZE)
    c_pair = swap_x(context[1])
    c_mine = context[0]
    context = jnp.concatenate(
        [jnp.where(mine == 0, c_mine, c_pair), jnp.where(mine == 0, c_pair, c_mine)], axis=0
    )
    context = jnp.concatenate([context, swap_core(context)], axis=0)
    context, wo_near = lax.optimization_barrier((context, wo_near))
    send = jnp.einsum(
        "td,gnd->gtn",
        context,
        wo_near.reshape(rows_y, rows_z * piece, -1),
        preferred_element_type=jnp.float32,
    ).astype(jnp.bfloat16)
    terms = lax.all_to_all(send, REP, split_axis=0, concat_axis=0, tiled=True)
    summed = jnp.sum(terms.astype(jnp.float32), axis=0).astype(jnp.bfloat16)
    near_cols = summed[: 2 * span].reshape(2 * span, rows_z, piece)
    far_cols = swap_core(summed[2 * span :]).reshape(2 * span, rows_z, piece)
    first = jnp.where(core == 0, near_cols, far_cols)
    second = jnp.where(core == 0, far_cols, near_cols)
    attn_out = jnp.stack([first, second], axis=2).reshape(2, 1, 2, blk, -1)
    new_cache = settle_pages(cache_pages, move_page, arrived)
    return (attn_out, new_cache)


def solution(mesh):
    ctx, rep = mesh.devices.shape
    fine = Mesh(mesh.devices.reshape(rep, ctx // rep // 2, 2, 2, rep // 2), CTX + REP)
    return jax.shard_map(
        on_device,
        mesh=fine,
        in_specs=(
            P(None, CTX, None, None, None),
            P(),
            P(CTX, REP),
            P(CTX, None),
            P(CTX, None),
            P(REP, CTX),
            P(),
            P(),
            P(CTX, REP, None, None, None),
            P(CTX, REP, None),
            P(CTX, REP, None),
            P(CTX, REP, None),
        ),
        out_specs=(P(None, CTX, None, None, REP), P(CTX, REP, None, None, None)),
        check_vma=False,
    )
```

```python
import math

import jax
import jax.numpy as jnp
from jax import lax
from jax.experimental import pallas as pl
from jax.experimental.pallas import tpu as pltpu
from jax.sharding import Mesh
from jax.sharding import PartitionSpec as P

HEAD_SIZE = 128
HEADS_PER_KV = 8

CTX = ("y", "zh", "core")
REP = ("zl", "x")
CHIPS = ("y", "zh")

rope_base = 5000000.0
neg_fill = -1e30


def rope_tables(positions):
    half = HEAD_SIZE // 2
    steps_f = jnp.arange(half, dtype=jnp.float32) * (2.0 / HEAD_SIZE)
    freq = jnp.exp(-steps_f * math.log(rope_base))
    angle = positions.astype(jnp.float32)[:, None] * freq[None, :]
    return (jnp.cos(angle), jnp.sin(angle))


def apply_rotation(values, cosine_table, sine_table):
    half = values.shape[-1] // 2
    first = values[..., :half]
    second = values[..., half:]
    cosine_table = cosine_table[:, None, :]
    sine_table = sine_table[:, None, :]
    return jnp.concatenate(
        [first * cosine_table - second * sine_table, second * cosine_table + first * sine_table],
        axis=-1,
    )


def matmul(left, right):
    return jnp.dot(left, right, preferred_element_type=jnp.float32)


def spread(block, axes):
    size = lax.axis_size(axes)
    copies = jnp.broadcast_to(block[None], (size,) + block.shape)
    return lax.all_to_all(copies, axes, split_axis=0, concat_axis=0, tiled=True)


def swap_core(value):
    return lax.ppermute(value, "core", [(0, 1), (1, 0)])


def swap_x(value):
    return lax.ppermute(value, "x", [(i, i ^ 1) for i in range(lax.axis_size("x"))])


def norm_kernel(core_ref, hidden_ref, gain_ref, near_ref, far_ref):
    hidden = hidden_ref[...].astype(jnp.float32)
    scale = lax.rsqrt(jnp.mean(hidden * hidden, axis=-1, keepdims=True) + 1e-05)
    normed = hidden * scale * gain_ref[...].astype(jnp.float32)
    core = core_ref[0]
    lane = lax.broadcasted_iota(jnp.int32, (hidden.shape[0], 128), 1)
    for pair in range(hidden.shape[1] // 256):
        left = normed[:, 256 * pair : 256 * pair + 128]
        right = normed[:, 256 * pair + 128 : 256 * pair + 256]
        even = jnp.where(lane < 64, left, pltpu.roll(right, 64, 1)).astype(jnp.bfloat16)
        odd = jnp.where(lane < 64, pltpu.roll(left, 64, 1), right).astype(jnp.bfloat16)
        span = slice(128 * pair, 128 * pair + 128)
        near_ref[:, span] = jnp.where(core == 0, even, odd)
        far_ref[:, span] = jnp.where(core == 0, odd, even)


def split_norm(hidden, gain, core):
    rows, width = hidden.shape
    tile = 32
    half = jax.ShapeDtypeStruct((rows, width // 2), jnp.bfloat16)
    half_spec = pl.BlockSpec((tile, width // 2), lambda i: (i, 0))
    return pl.pallas_call(
        norm_kernel,
        grid=(rows // tile,),
        in_specs=[
            pl.BlockSpec(memory_space=pltpu.SMEM),
            pl.BlockSpec((tile, width), lambda i: (i, 0)),
            pl.BlockSpec((1, width), lambda i: (0, 0)),
        ],
        out_specs=(half_spec, half_spec),
        out_shape=(half, half),
        name="split_norm",
    )(core.reshape(1), hidden, gain[None])


def attend_kernel(q_ref, near_ref, far_ref, qpos_ref, kpos_ref, out_ref):
    half = near_ref.shape[0]
    queries = q_ref[...]
    scores = []
    masks = []
    for part, ref in enumerate((near_ref, far_ref)):
        keys = ref[:, :HEAD_SIZE]
        raw = lax.dot_general(
            queries, keys, (((1,), (1,)), ((), ())), preferred_element_type=jnp.float32
        )
        raw = raw * HEAD_SIZE ** (-0.5)
        allowed = kpos_ref[:, part * half : (part + 1) * half] <= qpos_ref[...]
        scores.append(raw)
        masks.append(allowed)
    top = jnp.maximum(
        jnp.max(jnp.where(masks[0], scores[0], neg_fill), axis=-1, keepdims=True),
        jnp.max(jnp.where(masks[1], scores[1], neg_fill), axis=-1, keepdims=True),
    )
    total = jnp.zeros_like(top)
    acc = jnp.zeros(out_ref.shape, jnp.float32)
    for raw, allowed, ref in zip(scores, masks, (near_ref, far_ref)):
        weights = jnp.where(allowed, jnp.exp(raw - top), 0.0)
        total = total + jnp.sum(weights, axis=-1, keepdims=True)
        acc = acc + matmul(weights.astype(jnp.bfloat16), ref[:, HEAD_SIZE:])
    out_ref[...] = (acc / jnp.maximum(total, 1.0)).astype(jnp.bfloat16)


def attend(queries, near, far, qpos, kpos):
    rows, half = queries.shape[0], near.shape[0]
    tile = min(rows, 128)
    return pl.pallas_call(
        attend_kernel,
        grid=(rows // tile,),
        in_specs=[
            pl.BlockSpec((tile, HEAD_SIZE), lambda i: (i, 0)),
            pl.BlockSpec((half, 2 * HEAD_SIZE), lambda i: (0, 0)),
            pl.BlockSpec((half, 2 * HEAD_SIZE), lambda i: (0, 0)),
            pl.BlockSpec((tile, 1), lambda i: (i, 0)),
            pl.BlockSpec((1, 2 * half), lambda i: (0, 0)),
        ],
        out_specs=pl.BlockSpec((tile, HEAD_SIZE), lambda i: (i, 0)),
        out_shape=jax.ShapeDtypeStruct((rows, HEAD_SIZE), jnp.bfloat16),
        compiler_params=pltpu.CompilerParams(vmem_limit_bytes=40 << 20),
        name="attend",
    )(queries, near, far, qpos, kpos)


def pages_kernel(page_ref, dest_ref, slot_ref, cache_ref, send_ref):
    groups, moves = send_ref.shape[:2]
    free = cache_ref.shape[0] - moves
    leaving = [cache_ref[page_ref[move]] for move in range(moves)]
    for group in range(groups):
        for slot in range(moves):
            page = jnp.zeros_like(leaving[0])
            for move in range(moves):
                here = (dest_ref[move] == group) & (slot_ref[move] == free + slot)
                page = jnp.where(here, leaving[move], page)
            send_ref[group, slot] = page


def pages_to_send(cache_pages, move_page, move_dest, move_slot):
    pages = cache_pages[0, 0]
    shape = (lax.axis_size(REP), move_page.shape[2]) + pages.shape[1:]
    scalars = pl.BlockSpec(memory_space=pltpu.SMEM)
    vector = pl.BlockSpec(memory_space=pltpu.VMEM)
    return pl.pallas_call(
        pages_kernel,
        in_specs=[scalars, scalars, scalars, vector],
        out_specs=vector,
        out_shape=jax.ShapeDtypeStruct(shape, pages.dtype),
        name="pages_to_send",
    )(move_page[0, 0], move_dest[0, 0], move_slot[0, 0], pages)


def settle_pages(cache_pages, move_page, arrived):
    pages = cache_pages[0, 0]
    page_count = pages.shape[0]
    moves = move_page.shape[2]
    leave_ids = move_page[0, 0]
    gone = jnp.any(leave_ids[:, None] == jnp.arange(page_count, dtype=jnp.int32)[None, :], axis=0)
    kept = jnp.where(gone[:, None, None], jnp.zeros_like(pages), pages)
    new_pages = jnp.concatenate([kept[: page_count - moves], arrived[0]], axis=0)
    return new_pages.reshape(cache_pages.shape)


def on_device(
    hidden_in,
    norm_gain,
    w_query,
    key_matrix,
    value_matrix,
    w_out,
    prompt_len,
    pair_of_device,
    cache_pages,
    move_page,
    move_dest,
    move_slot,
):
    cycle = lax.axis_size(CTX)
    place = lax.axis_index(CTX)
    rank = lax.axis_index(REP)
    core = lax.axis_index("core")
    rows_y, rows_z = lax.axis_size("y"), lax.axis_size("zh")
    mine = lax.axis_index("x") % 2
    blk = hidden_in.shape[3]
    span = 2 * blk
    width = hidden_in.shape[4]
    piece = w_query.shape[0]
    heads_here = w_query.shape[1] // HEAD_SIZE
    kv_first = (rank * heads_here // HEADS_PER_KV) * HEAD_SIZE

    key_cols = lax.dynamic_slice_in_dim(key_matrix, kv_first, HEAD_SIZE, 1)
    value_cols = lax.dynamic_slice_in_dim(value_matrix, kv_first, HEAD_SIZE, 1)
    half_near = jnp.where(mine == 0, key_cols, value_cols)
    weights = jnp.concatenate([w_query, w_out.T, half_near], axis=1)
    weights = lax.all_gather(weights, "zh", axis=0, tiled=True)
    weights, leave = lax.optimization_barrier((weights, move_page))
    cols = w_query.shape[1]
    half_near = spread(weights[:, 2 * cols :], "y").reshape(-1, HEAD_SIZE)
    weights = lax.all_gather(weights[:, : 2 * cols], "y", axis=0, tiled=True)

    x_near, x_far = split_norm(hidden_in.reshape(2 * span, width), norm_gain, core)
    send_pages = pages_to_send(cache_pages, leave, move_dest, move_slot)
    arrived = lax.psum_scatter(send_pages, REP, scatter_dimension=0, tiled=True)
    x_other = swap_core(x_far)
    half_near, x_near, x_far = lax.optimization_barrier((half_near, x_near, x_far))
    half_far = swap_core(half_near)
    x_chip = jnp.concatenate([x_near, x_other], axis=0)

    own_pair = lax.dynamic_slice_in_dim(pair_of_device, place, 1, 1)[:, 0]
    blocks = jnp.stack([own_pair, 2 * cycle - 1 - own_pair], axis=1)
    qpos = (blocks[:, :, None] * blk + jnp.arange(blk, dtype=jnp.int32)).reshape(2, span)
    cosine_table, sine_table = rope_tables(qpos.reshape(-1))

    half = matmul(x_near, half_near) + matmul(x_far, half_far)
    keys = apply_rotation(half[:, None, :], cosine_table, sine_table)[:, 0]
    half = jnp.where(mine == 0, keys, half).astype(jnp.bfloat16).reshape(2, span, HEAD_SIZE)
    kept = lax.dynamic_index_in_dim(half, mine, 0, False)
    other = swap_x(lax.dynamic_index_in_dim(half, 1 - mine, 0, False))
    kv = jnp.where(
        mine == 0,
        jnp.concatenate([kept, other], axis=1),
        jnp.concatenate([other, kept], axis=1),
    )
    kv, x_chip = lax.optimization_barrier((kv, x_chip))
    near = spread(kv, CHIPS).reshape(-1, 2 * HEAD_SIZE)
    weights, arrived = lax.optimization_barrier((weights, arrived))
    query = matmul(x_chip, weights[:, :cols])
    query, weights = lax.optimization_barrier((query, weights))
    wo_near = weights[:, cols:]
    wo_far = swap_core(wo_near)
    query = query[: 2 * span] + swap_core(query[2 * span :])
    query = apply_rotation(
        query.reshape(2 * span, heads_here, HEAD_SIZE), cosine_table, sine_table
    ).astype(jnp.bfloat16)
    query = query.reshape(2, span, heads_here * HEAD_SIZE)
    q_mine = lax.dynamic_index_in_dim(query, mine, 0, False)
    q_send = lax.dynamic_index_in_dim(query, 1 - mine, 0, False)
    near, q_send = lax.optimization_barrier((near, q_send))
    far = swap_core(near)
    q_pair = swap_x(q_send)

    pairs = lax.dynamic_index_in_dim(pair_of_device, mine, 0, False).reshape(-1, 2)
    pairs = jnp.where(core == 0, pairs, pairs[:, ::-1]).T.reshape(-1)
    kblocks = jnp.stack([pairs, 2 * cycle - 1 - pairs], axis=1)
    kpos = (kblocks[..., None] * blk + jnp.arange(blk, dtype=jnp.int32)).reshape(1, -1)
    my_qpos = lax.dynamic_index_in_dim(qpos, mine, 0, False)
    my_len = lax.dynamic_index_in_dim(prompt_len, mine, 0, False)
    my_qpos = jnp.where(my_qpos < my_len, my_qpos, -1)
    all_q = jnp.stack([q_mine, q_pair]).reshape(-1, HEAD_SIZE)
    all_qpos = jnp.broadcast_to(my_qpos[None, :, None], (2, span, heads_here)).reshape(-1, 1)
    context = attend(all_q, near, far, all_qpos, kpos).reshape(2, span, heads_here * HEAD_SIZE)
    c_pair = swap_x(context[1])
    c_mine = context[0]
    context = jnp.concatenate(
        [jnp.where(mine == 0, c_mine, c_pair), jnp.where(mine == 0, c_pair, c_mine)], axis=0
    )

    def partial(weight):
        weight = weight.reshape(rows_y, rows_z * piece, -1)
        return jnp.einsum("td,gnd->gtn", context, weight, preferred_element_type=jnp.float32)

    send = jnp.concatenate([partial(wo_near), partial(wo_far)], axis=2).astype(jnp.bfloat16)
    terms = lax.all_to_all(send, REP, split_axis=0, concat_axis=0, tiled=True)
    summed = jnp.sum(terms.astype(jnp.float32), axis=0).astype(jnp.bfloat16)
    summed = summed.reshape(2 * span, 2, rows_z, piece)
    first = jnp.where(core == 0, summed[:, 0], summed[:, 1])
    second = jnp.where(core == 0, summed[:, 1], summed[:, 0])
    attn_out = jnp.stack([first, second], axis=2).reshape(2, 1, 2, blk, -1)
    new_cache = settle_pages(cache_pages, move_page, arrived)
    return (attn_out, new_cache)


def solution(mesh):
    ctx, rep = mesh.devices.shape
    fine = Mesh(mesh.devices.reshape(rep, ctx // rep // 2, 2, 2, rep // 2), CTX + REP)
    return jax.shard_map(
        on_device,
        mesh=fine,
        in_specs=(
            P(None, CTX, None, None, None),
            P(),
            P(CTX, REP),
            P(CTX, None),
            P(CTX, None),
            P(REP, CTX),
            P(),
            P(),
            P(CTX, REP, None, None, None),
            P(CTX, REP, None),
            P(CTX, REP, None),
            P(CTX, REP, None),
        ),
        out_specs=(P(None, CTX, None, None, REP), P(CTX, REP, None, None, None)),
        check_vma=False,
    )
```

```python
import math

import jax
import jax.numpy as jnp
from jax import lax
from jax.experimental import pallas as pl
from jax.experimental.pallas import tpu as pltpu
from jax.sharding import Mesh
from jax.sharding import PartitionSpec as P

HEAD_SIZE = 128
HEADS_PER_KV = 8

CTX = ("y", "zh", "core")
REP = ("zl", "xh", "xe")
SOURCES = ("y", "zh", "xe")

rope_base = 5000000.0
neg_fill = -1e30


def rope_tables(positions):
    half = HEAD_SIZE // 2
    steps_f = jnp.arange(half, dtype=jnp.float32) * (2.0 / HEAD_SIZE)
    freq = jnp.exp(-steps_f * math.log(rope_base))
    angle = positions.astype(jnp.float32)[:, None] * freq[None, :]
    return (jnp.cos(angle), jnp.sin(angle))


def apply_rotation(values, cosine_table, sine_table):
    half = values.shape[-1] // 2
    first = values[..., :half]
    second = values[..., half:]
    cosine_table = cosine_table[:, None, :]
    sine_table = sine_table[:, None, :]
    return jnp.concatenate(
        [first * cosine_table - second * sine_table, second * cosine_table + first * sine_table],
        axis=-1,
    )


def matmul(left, right):
    return jnp.dot(left, right, preferred_element_type=jnp.float32)


def exchange(blocks, axes):
    return lax.all_to_all(blocks, axes, split_axis=0, concat_axis=0, tiled=True)


def swap_core(value):
    return lax.ppermute(value, "core", [(0, 1), (1, 0)])


def swap_x(value):
    return lax.ppermute(value, "xe", [(0, 1), (1, 0)])


def norm_kernel(core_ref, hidden_ref, gain_ref, near_ref, far_ref):
    hidden = hidden_ref[...].astype(jnp.float32)
    scale = lax.rsqrt(jnp.mean(hidden * hidden, axis=-1, keepdims=True) + 1e-05)
    normed = hidden * scale * gain_ref[...].astype(jnp.float32)
    core = core_ref[0]
    lane = lax.broadcasted_iota(jnp.int32, (hidden.shape[0], 128), 1)
    for pair in range(hidden.shape[1] // 256):
        left = normed[:, 256 * pair : 256 * pair + 128]
        right = normed[:, 256 * pair + 128 : 256 * pair + 256]
        even = jnp.where(lane < 64, left, pltpu.roll(right, 64, 1)).astype(jnp.bfloat16)
        odd = jnp.where(lane < 64, pltpu.roll(left, 64, 1), right).astype(jnp.bfloat16)
        span = slice(128 * pair, 128 * pair + 128)
        near_ref[:, span] = jnp.where(core == 0, even, odd)
        far_ref[:, span] = jnp.where(core == 0, odd, even)


def split_norm(hidden, gain, core):
    rows, width = hidden.shape
    tile = 32
    half = jax.ShapeDtypeStruct((rows, width // 2), jnp.bfloat16)
    half_spec = pl.BlockSpec((tile, width // 2), lambda i: (i, 0))
    return pl.pallas_call(
        norm_kernel,
        grid=(rows // tile,),
        in_specs=[
            pl.BlockSpec(memory_space=pltpu.SMEM),
            pl.BlockSpec((tile, width), lambda i: (i, 0)),
            pl.BlockSpec((1, width), lambda i: (0, 0)),
        ],
        out_specs=(half_spec, half_spec),
        out_shape=(half, half),
        name="split_norm",
    )(core.reshape(1), hidden, gain[None])


def attend_kernel(q_ref, near_ref, far_ref, qpos_ref, kpos_ref, out_ref):
    half = near_ref.shape[0] * near_ref.shape[2]
    queries = q_ref[...]
    scores = []
    masks = []
    for part, ref in enumerate((near_ref, far_ref)):
        keys = ref[:, 0].reshape(half, HEAD_SIZE)
        raw = lax.dot_general(
            queries, keys, (((1,), (1,)), ((), ())), preferred_element_type=jnp.float32
        )
        raw = raw * HEAD_SIZE ** (-0.5)
        allowed = kpos_ref[:, part * half : (part + 1) * half] <= qpos_ref[...]
        scores.append(raw)
        masks.append(allowed)
    top = jnp.maximum(
        jnp.max(jnp.where(masks[0], scores[0], neg_fill), axis=-1, keepdims=True),
        jnp.max(jnp.where(masks[1], scores[1], neg_fill), axis=-1, keepdims=True),
    )
    total = jnp.zeros_like(top)
    acc = jnp.zeros(out_ref.shape, jnp.float32)
    for raw, allowed, ref in zip(scores, masks, (near_ref, far_ref)):
        weights = jnp.where(allowed, jnp.exp(raw - top), 0.0)
        total = total + jnp.sum(weights, axis=-1, keepdims=True)
        acc = acc + matmul(weights.astype(jnp.bfloat16), ref[:, 1].reshape(half, HEAD_SIZE))
    out_ref[...] = (acc / jnp.maximum(total, 1.0)).astype(jnp.bfloat16)


def attend(queries, near, far, qpos, kpos):
    rows, half = queries.shape[0], near.shape[0] * near.shape[2]
    tile = min(rows, 128)
    return pl.pallas_call(
        attend_kernel,
        grid=(rows // tile,),
        in_specs=[
            pl.BlockSpec((tile, HEAD_SIZE), lambda i: (i, 0)),
            pl.BlockSpec(near.shape, lambda i: (0, 0, 0, 0)),
            pl.BlockSpec(far.shape, lambda i: (0, 0, 0, 0)),
            pl.BlockSpec((tile, 1), lambda i: (i, 0)),
            pl.BlockSpec((1, 2 * half), lambda i: (0, 0)),
        ],
        out_specs=pl.BlockSpec((tile, HEAD_SIZE), lambda i: (i, 0)),
        out_shape=jax.ShapeDtypeStruct((rows, HEAD_SIZE), jnp.bfloat16),
        compiler_params=pltpu.CompilerParams(vmem_limit_bytes=40 << 20),
        name="attend",
    )(queries, near, far, qpos, kpos)


def pages_kernel(page_ref, dest_ref, slot_ref, cache_ref, send_ref):
    groups, moves = send_ref.shape[:2]
    free = cache_ref.shape[0] - moves
    leaving = [cache_ref[page_ref[move]] for move in range(moves)]
    for group in range(groups):
        for slot in range(moves):
            page = jnp.zeros_like(leaving[0])
            for move in range(moves):
                here = (dest_ref[move] == group) & (slot_ref[move] == free + slot)
                page = jnp.where(here, leaving[move], page)
            send_ref[group, slot] = page


def pages_to_send(cache_pages, move_page, move_dest, move_slot):
    pages = cache_pages[0, 0]
    shape = (lax.axis_size(REP), move_page.shape[2]) + pages.shape[1:]
    scalars = pl.BlockSpec(memory_space=pltpu.SMEM)
    vector = pl.BlockSpec(memory_space=pltpu.VMEM)
    return pl.pallas_call(
        pages_kernel,
        in_specs=[scalars, scalars, scalars, vector],
        out_specs=vector,
        out_shape=jax.ShapeDtypeStruct(shape, pages.dtype),
        name="pages_to_send",
    )(move_page[0, 0], move_dest[0, 0], move_slot[0, 0], pages)


def settle_pages(cache_pages, move_page, arrived):
    pages = cache_pages[0, 0]
    page_count = pages.shape[0]
    moves = move_page.shape[2]
    leave_ids = move_page[0, 0]
    gone = jnp.any(leave_ids[:, None] == jnp.arange(page_count, dtype=jnp.int32)[None, :], axis=0)
    kept = jnp.where(gone[:, None, None], jnp.zeros_like(pages), pages)
    new_pages = jnp.concatenate([kept[: page_count - moves], arrived[0]], axis=0)
    return new_pages.reshape(cache_pages.shape)


def on_device(
    hidden_in,
    norm_gain,
    w_query,
    key_matrix,
    value_matrix,
    w_out,
    prompt_len,
    pair_of_device,
    cache_pages,
    move_page,
    move_dest,
    move_slot,
):
    cycle = lax.axis_size(CTX)
    place = lax.axis_index(CTX)
    rank = lax.axis_index(REP)
    core = lax.axis_index("core")
    rows_y, rows_z = lax.axis_size("y"), lax.axis_size("zh")
    mine = lax.axis_index("xe")
    blk = hidden_in.shape[3]
    span = 2 * blk
    width = hidden_in.shape[4]
    piece = w_query.shape[0]
    heads_here = w_query.shape[1] // HEAD_SIZE
    kv_first = (rank * heads_here // HEADS_PER_KV) * HEAD_SIZE

    key_cols = lax.dynamic_slice_in_dim(key_matrix, kv_first, HEAD_SIZE, 1)
    value_cols = lax.dynamic_slice_in_dim(value_matrix, kv_first, HEAD_SIZE, 1)
    half_near = jnp.where(mine == 0, key_cols, value_cols)
    weights = jnp.concatenate([w_query, w_out.T, half_near], axis=1)
    weights = lax.all_gather(weights, "zh", axis=0, tiled=True)
    weights, leave = lax.optimization_barrier((weights, move_page))
    cols = w_query.shape[1]
    wq_near, wo_near = weights[:, :cols], weights[:, cols : 2 * cols]
    half_near = weights[:, 2 * cols :]
    half_near = exchange(jnp.broadcast_to(half_near[None], (rows_y,) + half_near.shape), "y")
    half_near = half_near.reshape(-1, HEAD_SIZE)
    wq_near = lax.all_gather(wq_near, "y", axis=0, tiled=True)

    x_near, x_far = split_norm(hidden_in.reshape(2 * span, width), norm_gain, core)
    send_pages = pages_to_send(cache_pages, leave, move_dest, move_slot)
    arrived = lax.psum_scatter(send_pages, REP, scatter_dimension=0, tiled=True)
    x_other = swap_core(x_far)
    half_near, x_near, x_far, wo_near = lax.optimization_barrier(
        (half_near, x_near, x_far, wo_near)
    )
    wo_near = lax.all_gather(wo_near, "y", axis=0, tiled=True)
    half_far = swap_core(half_near)
    x_chip = jnp.concatenate([x_near, x_other], axis=0)

    own_pair = lax.dynamic_slice_in_dim(pair_of_device, place, 1, 1)[:, 0]
    blocks = jnp.stack([own_pair, 2 * cycle - 1 - own_pair], axis=1)
    qpos = (blocks[:, :, None] * blk + jnp.arange(blk, dtype=jnp.int32)).reshape(2, span)
    cosine_table, sine_table = rope_tables(qpos.reshape(-1))

    half = matmul(x_near, half_near) + matmul(x_far, half_far)
    keys = apply_rotation(half[:, None, :], cosine_table, sine_table)[:, 0]
    half = jnp.where(mine == 0, keys, half).astype(jnp.bfloat16).reshape(2, span, HEAD_SIZE)
    half, x_chip = lax.optimization_barrier((half, x_chip))
    chips = rows_y * rows_z
    blocks = jnp.broadcast_to(half[None], (chips,) + half.shape)
    near = exchange(blocks.reshape(2 * chips, span, HEAD_SIZE), SOURCES)
    near = near.reshape(chips, 2, span, HEAD_SIZE)

    query = matmul(x_chip, wq_near)
    query = query[: 2 * span] + swap_core(query[2 * span :])
    query = apply_rotation(
        query.reshape(2 * span, heads_here, HEAD_SIZE), cosine_table, sine_table
    ).astype(jnp.bfloat16)
    query = query.reshape(2, span, heads_here * HEAD_SIZE)
    q_mine = lax.dynamic_index_in_dim(query, mine, 0, False)
    q_pair = swap_x(lax.dynamic_index_in_dim(query, 1 - mine, 0, False))

    pairs = lax.dynamic_index_in_dim(pair_of_device, mine, 0, False).reshape(-1, 2)
    pairs = jnp.where(core == 0, pairs, pairs[:, ::-1]).T.reshape(-1)
    kblocks = jnp.stack([pairs, 2 * cycle - 1 - pairs], axis=1)
    kpos = (kblocks[..., None] * blk + jnp.arange(blk, dtype=jnp.int32)).reshape(1, -1)
    my_qpos = lax.dynamic_index_in_dim(qpos, mine, 0, False)
    my_len = lax.dynamic_index_in_dim(prompt_len, mine, 0, False)
    my_qpos = jnp.where(my_qpos < my_len, my_qpos, -1)
    all_q = jnp.stack([q_mine, q_pair]).reshape(-1, HEAD_SIZE)
    near, all_q, arrived = lax.optimization_barrier((near, all_q, arrived))
    far = swap_core(near)
    all_qpos = jnp.broadcast_to(my_qpos[None, :, None], (2, span, heads_here)).reshape(-1, 1)
    context = attend(all_q, near, far, all_qpos, kpos).reshape(2, span, heads_here * HEAD_SIZE)
    c_pair = swap_x(context[1])
    c_mine = context[0]
    context = jnp.concatenate(
        [jnp.where(mine == 0, c_mine, c_pair), jnp.where(mine == 0, c_pair, c_mine)], axis=0
    )
    context = jnp.concatenate([context, swap_core(context)], axis=0)
    context, wo_near = lax.optimization_barrier((context, wo_near))
    send = jnp.einsum(
        "td,gnd->gtn",
        context,
        wo_near.reshape(rows_y, rows_z * piece, -1),
        preferred_element_type=jnp.float32,
    ).astype(jnp.bfloat16)
    terms = lax.all_to_all(send, REP, split_axis=0, concat_axis=0, tiled=True)
    summed = jnp.sum(terms.astype(jnp.float32), axis=0).astype(jnp.bfloat16)
    near_cols = summed[: 2 * span].reshape(2 * span, rows_z, piece)
    far_cols = swap_core(summed[2 * span :]).reshape(2 * span, rows_z, piece)
    first = jnp.where(core == 0, near_cols, far_cols)
    second = jnp.where(core == 0, far_cols, near_cols)
    attn_out = jnp.stack([first, second], axis=2).reshape(2, 1, 2, blk, -1)
    new_cache = settle_pages(cache_pages, move_page, arrived)
    return (attn_out, new_cache)


def solution(mesh):
    ctx, rep = mesh.devices.shape
    fine = Mesh(mesh.devices.reshape(rep, ctx // rep // 2, 2, 2, rep // 4, 2), CTX + REP)
    return jax.shard_map(
        on_device,
        mesh=fine,
        in_specs=(
            P(None, CTX, None, None, None),
            P(),
            P(CTX, REP),
            P(CTX, None),
            P(CTX, None),
            P(REP, CTX),
            P(),
            P(),
            P(CTX, REP, None, None, None),
            P(CTX, REP, None),
            P(CTX, REP, None),
            P(CTX, REP, None),
        ),
        out_specs=(P(None, CTX, None, None, REP), P(CTX, REP, None, None, None)),
        check_vma=False,
    )
```

```python
import math

import jax
import jax.numpy as jnp
from jax import lax
from jax.experimental import pallas as pl
from jax.experimental.pallas import tpu as pltpu
from jax.sharding import Mesh
from jax.sharding import PartitionSpec as P

HEAD_SIZE = 128
HEADS_PER_KV = 8

CTX = ("y", "zh", "core")
REP = ("zl", "x")
CHIPS = ("y", "zh")

rope_base = 5000000.0
neg_fill = -1e30


def rope_tables(positions):
    half = HEAD_SIZE // 2
    steps_f = jnp.arange(half, dtype=jnp.float32) * (2.0 / HEAD_SIZE)
    freq = jnp.exp(-steps_f * math.log(rope_base))
    angle = positions.astype(jnp.float32)[:, None] * freq[None, :]
    return (jnp.cos(angle), jnp.sin(angle))


def apply_rotation(values, cosine_table, sine_table):
    half = values.shape[-1] // 2
    first = values[..., :half]
    second = values[..., half:]
    cosine_table = cosine_table[:, None, :]
    sine_table = sine_table[:, None, :]
    return jnp.concatenate(
        [first * cosine_table - second * sine_table, second * cosine_table + first * sine_table],
        axis=-1,
    )


def matmul(left, right):
    return jnp.dot(left, right, preferred_element_type=jnp.float32)


def spread(block, axes):
    size = lax.axis_size(axes)
    copies = jnp.broadcast_to(block[None], (size,) + block.shape)
    return lax.all_to_all(copies, axes, split_axis=0, concat_axis=0, tiled=True)


def swap_core(value):
    return lax.ppermute(value, "core", [(0, 1), (1, 0)])


def swap_x(value):
    return lax.ppermute(value, "x", [(i, i ^ 1) for i in range(lax.axis_size("x"))])


def norm_kernel(core_ref, hidden_ref, gain_ref, near_ref, far_ref):
    hidden = hidden_ref[...].astype(jnp.float32)
    scale = lax.rsqrt(jnp.mean(hidden * hidden, axis=-1, keepdims=True) + 1e-05)
    normed = hidden * scale * gain_ref[...].astype(jnp.float32)
    core = core_ref[0]
    lane = lax.broadcasted_iota(jnp.int32, (hidden.shape[0], 128), 1)
    for pair in range(hidden.shape[1] // 256):
        left = normed[:, 256 * pair : 256 * pair + 128]
        right = normed[:, 256 * pair + 128 : 256 * pair + 256]
        even = jnp.where(lane < 64, left, pltpu.roll(right, 64, 1)).astype(jnp.bfloat16)
        odd = jnp.where(lane < 64, pltpu.roll(left, 64, 1), right).astype(jnp.bfloat16)
        span = slice(128 * pair, 128 * pair + 128)
        near_ref[:, span] = jnp.where(core == 0, even, odd)
        far_ref[:, span] = jnp.where(core == 0, odd, even)


def split_norm(hidden, gain, core):
    rows, width = hidden.shape
    tile = 32
    half = jax.ShapeDtypeStruct((rows, width // 2), jnp.bfloat16)
    half_spec = pl.BlockSpec((tile, width // 2), lambda i: (i, 0))
    return pl.pallas_call(
        norm_kernel,
        grid=(rows // tile,),
        in_specs=[
            pl.BlockSpec(memory_space=pltpu.SMEM),
            pl.BlockSpec((tile, width), lambda i: (i, 0)),
            pl.BlockSpec((1, width), lambda i: (0, 0)),
        ],
        out_specs=(half_spec, half_spec),
        out_shape=(half, half),
        compiler_params=pltpu.CompilerParams(vmem_limit_bytes=12 << 20),
        name="split_norm",
    )(core.reshape(1), hidden, gain[None])


def attend_kernel(q_ref, near_ref, far_ref, qpos_ref, kpos_ref, out_ref):
    half = near_ref.shape[0]
    queries = q_ref[...]
    scores = []
    masks = []
    for part, ref in enumerate((near_ref, far_ref)):
        keys = ref[:, :HEAD_SIZE]
        raw = lax.dot_general(
            queries, keys, (((1,), (1,)), ((), ())), preferred_element_type=jnp.float32
        )
        raw = raw * HEAD_SIZE ** (-0.5)
        allowed = kpos_ref[:, part * half : (part + 1) * half] <= qpos_ref[...]
        scores.append(raw)
        masks.append(allowed)
    top = jnp.maximum(
        jnp.max(jnp.where(masks[0], scores[0], neg_fill), axis=-1, keepdims=True),
        jnp.max(jnp.where(masks[1], scores[1], neg_fill), axis=-1, keepdims=True),
    )
    total = jnp.zeros_like(top)
    acc = jnp.zeros(out_ref.shape, jnp.float32)
    for raw, allowed, ref in zip(scores, masks, (near_ref, far_ref)):
        weights = jnp.where(allowed, jnp.exp(raw - top), 0.0)
        total = total + jnp.sum(weights, axis=-1, keepdims=True)
        acc = acc + matmul(weights.astype(jnp.bfloat16), ref[:, HEAD_SIZE:])
    out_ref[...] = (acc / jnp.maximum(total, 1.0)).astype(jnp.bfloat16)


def attend(queries, near, far, qpos, kpos):
    rows, half = queries.shape[0], near.shape[0]
    tile = min(rows, 128)
    return pl.pallas_call(
        attend_kernel,
        grid=(rows // tile,),
        in_specs=[
            pl.BlockSpec((tile, HEAD_SIZE), lambda i: (i, 0)),
            pl.BlockSpec((half, 2 * HEAD_SIZE), lambda i: (0, 0)),
            pl.BlockSpec((half, 2 * HEAD_SIZE), lambda i: (0, 0)),
            pl.BlockSpec((tile, 1), lambda i: (i, 0)),
            pl.BlockSpec((1, 2 * half), lambda i: (0, 0)),
        ],
        out_specs=pl.BlockSpec((tile, HEAD_SIZE), lambda i: (i, 0)),
        out_shape=jax.ShapeDtypeStruct((rows, HEAD_SIZE), jnp.bfloat16),
        compiler_params=pltpu.CompilerParams(vmem_limit_bytes=40 << 20),
        name="attend",
    )(queries, near, far, qpos, kpos)


def project_kernel(context_ref, weight_ref, out_ref):
    out_ref[0] = lax.dot_general(
        context_ref[...],
        weight_ref[...],
        (((1,), (1,)), ((), ())),
        preferred_element_type=jnp.float32,
    ).astype(jnp.bfloat16)


def project(context, weight, groups):
    rows, width = context.shape
    cols = weight.shape[0] // groups
    return pl.pallas_call(
        project_kernel,
        grid=(groups,),
        in_specs=[
            pl.BlockSpec((rows, width), lambda i: (0, 0)),
            pl.BlockSpec((cols, width), lambda i: (i, 0)),
        ],
        out_specs=pl.BlockSpec((1, rows, cols), lambda i: (i, 0, 0)),
        out_shape=jax.ShapeDtypeStruct((groups, rows, cols), jnp.bfloat16),
        name="project",
    )(context, weight)


def weave_kernel(core_ref, near_ref, far_ref, out_ref):
    core = core_ref[0]
    lane = lax.broadcasted_iota(jnp.int32, (near_ref.shape[0], 128), 1)
    for pair in range(near_ref.shape[1] // 128):
        span = slice(128 * pair, 128 * pair + 128)
        near = near_ref[:, span].astype(jnp.float32)
        far = far_ref[:, span].astype(jnp.float32)
        first = jnp.where(core == 0, near, far)
        second = jnp.where(core == 0, far, near)
        low = jnp.where(lane < 64, first, pltpu.roll(second, 64, 1))
        high = jnp.where(lane < 64, pltpu.roll(first, 64, 1), second)
        out_ref[:, 256 * pair : 256 * pair + 128] = low.astype(jnp.bfloat16)
        out_ref[:, 256 * pair + 128 : 256 * pair + 256] = high.astype(jnp.bfloat16)


def weave(near, far, core):
    rows, cols = near.shape
    half = pl.BlockSpec((rows, cols), lambda i: (0, 0))
    return pl.pallas_call(
        weave_kernel,
        grid=(1,),
        in_specs=[pl.BlockSpec(memory_space=pltpu.SMEM), half, half],
        out_specs=pl.BlockSpec((rows, 2 * cols), lambda i: (0, 0)),
        out_shape=jax.ShapeDtypeStruct((rows, 2 * cols), near.dtype),
        compiler_params=pltpu.CompilerParams(vmem_limit_bytes=12 << 20),
        name="weave",
    )(core.reshape(1), near, far)


def pages_kernel(page_ref, dest_ref, slot_ref, cache_ref, send_ref):
    groups, moves = send_ref.shape[:2]
    free = cache_ref.shape[0] - moves
    leaving = [cache_ref[page_ref[move]] for move in range(moves)]
    for group in range(groups):
        for slot in range(moves):
            page = jnp.zeros_like(leaving[0])
            for move in range(moves):
                here = (dest_ref[move] == group) & (slot_ref[move] == free + slot)
                page = jnp.where(here, leaving[move], page)
            send_ref[group, slot] = page


def pages_to_send(cache_pages, move_page, move_dest, move_slot):
    pages = cache_pages[0, 0]
    shape = (lax.axis_size(REP), move_page.shape[2]) + pages.shape[1:]
    scalars = pl.BlockSpec(memory_space=pltpu.SMEM)
    vector = pl.BlockSpec(memory_space=pltpu.VMEM)
    return pl.pallas_call(
        pages_kernel,
        in_specs=[scalars, scalars, scalars, vector],
        out_specs=vector,
        out_shape=jax.ShapeDtypeStruct(shape, pages.dtype),
        compiler_params=pltpu.CompilerParams(vmem_limit_bytes=12 << 20),
        name="pages_to_send",
    )(move_page[0, 0], move_dest[0, 0], move_slot[0, 0], pages)


def settle_pages(cache_pages, move_page, arrived):
    pages = cache_pages[0, 0]
    page_count = pages.shape[0]
    moves = move_page.shape[2]
    leave_ids = move_page[0, 0]
    gone = jnp.any(leave_ids[:, None] == jnp.arange(page_count, dtype=jnp.int32)[None, :], axis=0)
    kept = jnp.where(gone[:, None, None], jnp.zeros_like(pages), pages)
    new_pages = jnp.concatenate([kept[: page_count - moves], arrived[0]], axis=0)
    return new_pages.reshape(cache_pages.shape)


def on_device(
    hidden_in,
    norm_gain,
    w_query,
    key_matrix,
    value_matrix,
    w_out,
    prompt_len,
    pair_of_device,
    cache_pages,
    move_page,
    move_dest,
    move_slot,
):
    cycle = lax.axis_size(CTX)
    place = lax.axis_index(CTX)
    rank = lax.axis_index(REP)
    core = lax.axis_index("core")
    rows_y, rows_z = lax.axis_size("y"), lax.axis_size("zh")
    mine = lax.axis_index("x") % 2
    blk = hidden_in.shape[3]
    span = 2 * blk
    width = hidden_in.shape[4]
    piece = w_query.shape[0]
    heads_here = w_query.shape[1] // HEAD_SIZE
    kv_first = (rank * heads_here // HEADS_PER_KV) * HEAD_SIZE

    key_cols = lax.dynamic_slice_in_dim(key_matrix, kv_first, HEAD_SIZE, 1)
    value_cols = lax.dynamic_slice_in_dim(value_matrix, kv_first, HEAD_SIZE, 1)
    half_near = jnp.where(mine == 0, key_cols, value_cols)
    weights = jnp.concatenate([w_query, w_out.T, half_near], axis=1)
    weights = lax.all_gather(weights, "zh", axis=0, tiled=True)
    weights, leave = lax.optimization_barrier((weights, move_page))
    cols = w_query.shape[1]
    wq_near, wo_near = weights[:, :cols], weights[:, cols : 2 * cols]
    half_near = spread(weights[:, 2 * cols :], "y").reshape(-1, HEAD_SIZE)
    wq_near = lax.all_gather(wq_near, "y", axis=0, tiled=True)

    x_near, x_far = split_norm(hidden_in.reshape(2 * span, width), norm_gain, core)
    send_pages = pages_to_send(cache_pages, leave, move_dest, move_slot)
    arrived = lax.psum_scatter(send_pages, REP, scatter_dimension=0, tiled=True)
    x_other = swap_core(x_far)
    half_near, x_near, x_far, wo_near = lax.optimization_barrier(
        (half_near, x_near, x_far, wo_near)
    )
    wo_near = lax.all_gather(wo_near, "y", axis=0, tiled=True)
    half_far = swap_core(half_near)
    x_chip = jnp.concatenate([x_near, x_other], axis=0)

    own_pair = lax.dynamic_slice_in_dim(pair_of_device, place, 1, 1)[:, 0]
    blocks = jnp.stack([own_pair, 2 * cycle - 1 - own_pair], axis=1)
    qpos = (blocks[:, :, None] * blk + jnp.arange(blk, dtype=jnp.int32)).reshape(2, span)
    cosine_table, sine_table = rope_tables(qpos.reshape(-1))

    half = matmul(x_near, half_near) + matmul(x_far, half_far)
    keys = apply_rotation(half[:, None, :], cosine_table, sine_table)[:, 0]
    half = jnp.where(mine == 0, keys, half).astype(jnp.bfloat16).reshape(2, span, HEAD_SIZE)
    kept = lax.dynamic_index_in_dim(half, mine, 0, False)
    other = swap_x(lax.dynamic_index_in_dim(half, 1 - mine, 0, False))
    kv = jnp.where(
        mine == 0,
        jnp.concatenate([kept, other], axis=1),
        jnp.concatenate([other, kept], axis=1),
    )
    kv, x_chip = lax.optimization_barrier((kv, x_chip))
    near = spread(kv, CHIPS).reshape(-1, 2 * HEAD_SIZE)
    query = matmul(x_chip, wq_near)
    query = query[: 2 * span] + swap_core(query[2 * span :])
    query = apply_rotation(
        query.reshape(2 * span, heads_here, HEAD_SIZE), cosine_table, sine_table
    ).astype(jnp.bfloat16)
    query = query.reshape(2, span, heads_here * HEAD_SIZE)
    q_mine = lax.dynamic_index_in_dim(query, mine, 0, False)
    q_pair = swap_x(lax.dynamic_index_in_dim(query, 1 - mine, 0, False))

    pairs = lax.dynamic_index_in_dim(pair_of_device, mine, 0, False).reshape(-1, 2)
    pairs = jnp.where(core == 0, pairs, pairs[:, ::-1]).T.reshape(-1)
    kblocks = jnp.stack([pairs, 2 * cycle - 1 - pairs], axis=1)
    kpos = (kblocks[..., None] * blk + jnp.arange(blk, dtype=jnp.int32)).reshape(1, -1)
    my_qpos = lax.dynamic_index_in_dim(qpos, mine, 0, False)
    my_len = lax.dynamic_index_in_dim(prompt_len, mine, 0, False)
    my_qpos = jnp.where(my_qpos < my_len, my_qpos, -1)
    all_q = jnp.stack([q_mine, q_pair]).reshape(-1, HEAD_SIZE)
    near, all_q, arrived = lax.optimization_barrier((near, all_q, arrived))
    far = swap_core(near)
    all_qpos = jnp.broadcast_to(my_qpos[None, :, None], (2, span, heads_here)).reshape(-1, 1)
    context = attend(all_q, near, far, all_qpos, kpos).reshape(2, span, heads_here * HEAD_SIZE)
    c_pair = swap_x(context[1])
    c_mine = context[0]
    context = jnp.concatenate(
        [jnp.where(mine == 0, c_mine, c_pair), jnp.where(mine == 0, c_pair, c_mine)], axis=0
    )
    context = jnp.concatenate([context, swap_core(context)], axis=0)
    context, wo_near = lax.optimization_barrier((context, wo_near))
    send = project(context, wo_near, rows_y)
    terms = lax.all_to_all(send, REP, split_axis=0, concat_axis=0, tiled=True)
    summed = jnp.sum(terms.astype(jnp.float32), axis=0).astype(jnp.bfloat16)
    attn_out = weave(summed[: 2 * span], swap_core(summed[2 * span :]), core)
    attn_out = attn_out.reshape(2, 1, 2, blk, -1)
    new_cache = settle_pages(cache_pages, move_page, arrived)
    return (attn_out, new_cache)


def solution(mesh):
    ctx, rep = mesh.devices.shape
    fine = Mesh(mesh.devices.reshape(rep, ctx // rep // 2, 2, 2, rep // 2), CTX + REP)
    return jax.shard_map(
        on_device,
        mesh=fine,
        in_specs=(
            P(None, CTX, None, None, None),
            P(),
            P(CTX, REP),
            P(CTX, None),
            P(CTX, None),
            P(REP, CTX),
            P(),
            P(),
            P(CTX, REP, None, None, None),
            P(CTX, REP, None),
            P(CTX, REP, None),
            P(CTX, REP, None),
        ),
        out_specs=(P(None, CTX, None, None, REP), P(CTX, REP, None, None, None)),
        check_vma=False,
    )
```

```python
import math

import jax
import jax.numpy as jnp
from jax import lax
from jax.experimental import pallas as pl
from jax.experimental.pallas import tpu as pltpu
from jax.sharding import Mesh
from jax.sharding import PartitionSpec as P

HEAD_SIZE = 128
HEADS_PER_KV = 8

CTX = ("y", "zh", "core")
REP = ("zl", "x")
CHIPS = ("y", "zh")

rope_base = 5000000.0
neg_fill = -1e30


def rope_tables(positions):
    half = HEAD_SIZE // 2
    steps_f = jnp.arange(half, dtype=jnp.float32) * (2.0 / HEAD_SIZE)
    freq = jnp.exp(-steps_f * math.log(rope_base))
    angle = positions.astype(jnp.float32)[:, None] * freq[None, :]
    return (jnp.cos(angle), jnp.sin(angle))


def apply_rotation(values, cosine_table, sine_table):
    half = values.shape[-1] // 2
    first = values[..., :half]
    second = values[..., half:]
    cosine_table = cosine_table[:, None, :]
    sine_table = sine_table[:, None, :]
    return jnp.concatenate(
        [first * cosine_table - second * sine_table, second * cosine_table + first * sine_table],
        axis=-1,
    )


def matmul(left, right):
    return jnp.dot(left, right, preferred_element_type=jnp.float32)


def spread(block, axes):
    size = lax.axis_size(axes)
    copies = jnp.broadcast_to(block[None], (size,) + block.shape)
    return lax.all_to_all(copies, axes, split_axis=0, concat_axis=0, tiled=True)


def swap_core(value):
    return lax.ppermute(value, "core", [(0, 1), (1, 0)])


def swap_x(value):
    return lax.ppermute(value, "x", [(i, i ^ 1) for i in range(lax.axis_size("x"))])


def norm_kernel(core_ref, hidden_ref, gain_ref, near_ref, far_ref):
    hidden = hidden_ref[...].astype(jnp.float32)
    scale = lax.rsqrt(jnp.mean(hidden * hidden, axis=-1, keepdims=True) + 1e-05)
    normed = hidden * scale * gain_ref[...].astype(jnp.float32)
    core = core_ref[0]
    lane = lax.broadcasted_iota(jnp.int32, (hidden.shape[0], 128), 1)
    for pair in range(hidden.shape[1] // 256):
        left = normed[:, 256 * pair : 256 * pair + 128]
        right = normed[:, 256 * pair + 128 : 256 * pair + 256]
        even = jnp.where(lane < 64, left, pltpu.roll(right, 64, 1)).astype(jnp.bfloat16)
        odd = jnp.where(lane < 64, pltpu.roll(left, 64, 1), right).astype(jnp.bfloat16)
        span = slice(128 * pair, 128 * pair + 128)
        near_ref[:, span] = jnp.where(core == 0, even, odd)
        far_ref[:, span] = jnp.where(core == 0, odd, even)


def split_norm(hidden, gain, core):
    rows, width = hidden.shape
    tile = 32
    half = jax.ShapeDtypeStruct((rows, width // 2), jnp.bfloat16)
    half_spec = pl.BlockSpec((tile, width // 2), lambda i: (i, 0))
    return pl.pallas_call(
        norm_kernel,
        grid=(rows // tile,),
        in_specs=[
            pl.BlockSpec(memory_space=pltpu.SMEM),
            pl.BlockSpec((tile, width), lambda i: (i, 0)),
            pl.BlockSpec((1, width), lambda i: (0, 0)),
        ],
        out_specs=(half_spec, half_spec),
        out_shape=(half, half),
        compiler_params=pltpu.CompilerParams(vmem_limit_bytes=12 << 20),
        name="split_norm",
    )(core.reshape(1), hidden, gain[None])


def attend_kernel(q_ref, near_ref, far_ref, qpos_ref, kpos_ref, out_ref):
    half = near_ref.shape[0]
    queries = q_ref[...]
    scores = []
    masks = []
    for part, ref in enumerate((near_ref, far_ref)):
        keys = ref[:, :HEAD_SIZE]
        raw = lax.dot_general(
            queries, keys, (((1,), (1,)), ((), ())), preferred_element_type=jnp.float32
        )
        raw = raw * HEAD_SIZE ** (-0.5)
        allowed = kpos_ref[:, part * half : (part + 1) * half] <= qpos_ref[...]
        scores.append(raw)
        masks.append(allowed)
    top = jnp.maximum(
        jnp.max(jnp.where(masks[0], scores[0], neg_fill), axis=-1, keepdims=True),
        jnp.max(jnp.where(masks[1], scores[1], neg_fill), axis=-1, keepdims=True),
    )
    total = jnp.zeros_like(top)
    acc = jnp.zeros(out_ref.shape, jnp.float32)
    for raw, allowed, ref in zip(scores, masks, (near_ref, far_ref)):
        weights = jnp.where(allowed, jnp.exp(raw - top), 0.0)
        total = total + jnp.sum(weights, axis=-1, keepdims=True)
        acc = acc + matmul(weights.astype(jnp.bfloat16), ref[:, HEAD_SIZE:])
    out_ref[...] = (acc / jnp.maximum(total, 1.0)).astype(jnp.bfloat16)


def attend(queries, near, far, qpos, kpos):
    rows, half = queries.shape[0], near.shape[0]
    tile = min(rows, 128)
    return pl.pallas_call(
        attend_kernel,
        grid=(rows // tile,),
        in_specs=[
            pl.BlockSpec((tile, HEAD_SIZE), lambda i: (i, 0)),
            pl.BlockSpec((half, 2 * HEAD_SIZE), lambda i: (0, 0)),
            pl.BlockSpec((half, 2 * HEAD_SIZE), lambda i: (0, 0)),
            pl.BlockSpec((tile, 1), lambda i: (i, 0)),
            pl.BlockSpec((1, 2 * half), lambda i: (0, 0)),
        ],
        out_specs=pl.BlockSpec((tile, HEAD_SIZE), lambda i: (i, 0)),
        out_shape=jax.ShapeDtypeStruct((rows, HEAD_SIZE), jnp.bfloat16),
        compiler_params=pltpu.CompilerParams(vmem_limit_bytes=40 << 20),
        name="attend",
    )(queries, near, far, qpos, kpos)


def pages_kernel(page_ref, dest_ref, slot_ref, cache_ref, send_ref):
    groups, moves = send_ref.shape[:2]
    free = cache_ref.shape[0] - moves
    leaving = [cache_ref[page_ref[move]] for move in range(moves)]
    for group in range(groups):
        for slot in range(moves):
            page = jnp.zeros_like(leaving[0])
            for move in range(moves):
                here = (dest_ref[move] == group) & (slot_ref[move] == free + slot)
                page = jnp.where(here, leaving[move], page)
            send_ref[group, slot] = page


def pages_to_send(cache_pages, move_page, move_dest, move_slot):
    pages = cache_pages[0, 0]
    shape = (lax.axis_size(REP), move_page.shape[2]) + pages.shape[1:]
    scalars = pl.BlockSpec(memory_space=pltpu.SMEM)
    vector = pl.BlockSpec(memory_space=pltpu.VMEM)
    return pl.pallas_call(
        pages_kernel,
        in_specs=[scalars, scalars, scalars, vector],
        out_specs=vector,
        out_shape=jax.ShapeDtypeStruct(shape, pages.dtype),
        compiler_params=pltpu.CompilerParams(vmem_limit_bytes=12 << 20),
        name="pages_to_send",
    )(move_page[0, 0], move_dest[0, 0], move_slot[0, 0], pages)


def settle_pages(cache_pages, move_page, arrived):
    pages = cache_pages[0, 0]
    page_count = pages.shape[0]
    moves = move_page.shape[2]
    leave_ids = move_page[0, 0]
    gone = jnp.any(leave_ids[:, None] == jnp.arange(page_count, dtype=jnp.int32)[None, :], axis=0)
    kept = jnp.where(gone[:, None, None], jnp.zeros_like(pages), pages)
    new_pages = jnp.concatenate([kept[: page_count - moves], arrived[0]], axis=0)
    return new_pages.reshape(cache_pages.shape)


def on_device(
    hidden_in,
    norm_gain,
    w_query,
    key_matrix,
    value_matrix,
    w_out,
    prompt_len,
    pair_of_device,
    cache_pages,
    move_page,
    move_dest,
    move_slot,
):
    cycle = lax.axis_size(CTX)
    place = lax.axis_index(CTX)
    rank = lax.axis_index(REP)
    core = lax.axis_index("core")
    rows_y, rows_z = lax.axis_size("y"), lax.axis_size("zh")
    mine = lax.axis_index("x") % 2
    blk = hidden_in.shape[3]
    span = 2 * blk
    width = hidden_in.shape[4]
    piece = w_query.shape[0]
    heads_here = w_query.shape[1] // HEAD_SIZE
    kv_first = (rank * heads_here // HEADS_PER_KV) * HEAD_SIZE

    key_cols = lax.dynamic_slice_in_dim(key_matrix, kv_first, HEAD_SIZE, 1)
    value_cols = lax.dynamic_slice_in_dim(value_matrix, kv_first, HEAD_SIZE, 1)
    half_near = jnp.where(mine == 0, key_cols, value_cols)
    weights = jnp.concatenate([w_query, w_out.T, half_near], axis=1)
    weights = lax.all_gather(weights, "zh", axis=0, tiled=True)
    weights, leave = lax.optimization_barrier((weights, move_page))
    cols = w_query.shape[1]
    wq_near, wo_near = weights[:, :cols], weights[:, cols : 2 * cols]
    half_near = spread(weights[:, 2 * cols :], "y").reshape(-1, HEAD_SIZE)
    wq_near = lax.all_gather(wq_near, "y", axis=0, tiled=True)

    x_near, x_far = split_norm(hidden_in.reshape(2 * span, width), norm_gain, core)
    send_pages = pages_to_send(cache_pages, leave, move_dest, move_slot)
    arrived = lax.psum_scatter(send_pages, REP, scatter_dimension=0, tiled=True)
    x_other = swap_core(x_far)
    half_near, x_near, x_far, wo_near = lax.optimization_barrier(
        (half_near, x_near, x_far, wo_near)
    )
    wo_near = lax.all_gather(wo_near, "y", axis=0, tiled=True)
    half_far = swap_core(half_near)
    x_chip = jnp.concatenate([x_near, x_other], axis=0)

    own_pair = lax.dynamic_slice_in_dim(pair_of_device, place, 1, 1)[:, 0]
    blocks = jnp.stack([own_pair, 2 * cycle - 1 - own_pair], axis=1)
    qpos = (blocks[:, :, None] * blk + jnp.arange(blk, dtype=jnp.int32)).reshape(2, span)
    cosine_table, sine_table = rope_tables(qpos.reshape(-1))

    half = matmul(x_near, half_near) + matmul(x_far, half_far)
    keys = apply_rotation(half[:, None, :], cosine_table, sine_table)[:, 0]
    half = jnp.where(mine == 0, keys, half).astype(jnp.bfloat16).reshape(2, span, HEAD_SIZE)
    kept = lax.dynamic_index_in_dim(half, mine, 0, False)
    other = swap_x(lax.dynamic_index_in_dim(half, 1 - mine, 0, False))
    kv = jnp.where(
        mine == 0,
        jnp.concatenate([kept, other], axis=1),
        jnp.concatenate([other, kept], axis=1),
    )
    kv, x_chip = lax.optimization_barrier((kv, x_chip))
    near = spread(kv, CHIPS).reshape(-1, 2 * HEAD_SIZE)
    query = matmul(x_chip, wq_near)
    query = query[: 2 * span] + swap_core(query[2 * span :])
    query = apply_rotation(
        query.reshape(2 * span, heads_here, HEAD_SIZE), cosine_table, sine_table
    ).astype(jnp.bfloat16)
    query = query.reshape(2, span, heads_here * HEAD_SIZE)
    q_mine = lax.dynamic_index_in_dim(query, mine, 0, False)
    q_pair = swap_x(lax.dynamic_index_in_dim(query, 1 - mine, 0, False))

    pairs = lax.dynamic_index_in_dim(pair_of_device, mine, 0, False).reshape(-1, 2)
    pairs = jnp.where(core == 0, pairs, pairs[:, ::-1]).T.reshape(-1)
    kblocks = jnp.stack([pairs, 2 * cycle - 1 - pairs], axis=1)
    kpos = (kblocks[..., None] * blk + jnp.arange(blk, dtype=jnp.int32)).reshape(1, -1)
    my_qpos = lax.dynamic_index_in_dim(qpos, mine, 0, False)
    my_len = lax.dynamic_index_in_dim(prompt_len, mine, 0, False)
    my_qpos = jnp.where(my_qpos < my_len, my_qpos, -1)
    all_q = jnp.stack([q_mine, q_pair]).reshape(-1, HEAD_SIZE)
    near, all_q, arrived = lax.optimization_barrier((near, all_q, arrived))
    far = swap_core(near)
    all_qpos = jnp.broadcast_to(my_qpos[None, :, None], (2, span, heads_here)).reshape(-1, 1)
    context = attend(all_q, near, far, all_qpos, kpos).reshape(2, span, heads_here * HEAD_SIZE)
    c_pair = swap_x(context[1])
    c_mine = context[0]
    context = jnp.concatenate(
        [jnp.where(mine == 0, c_mine, c_pair), jnp.where(mine == 0, c_pair, c_mine)], axis=0
    )
    context = jnp.concatenate([context, swap_core(context)], axis=0)
    context, wo_near = lax.optimization_barrier((context, wo_near))
    send = jnp.einsum(
        "td,gnd->gtn",
        context,
        wo_near.reshape(rows_y, rows_z * piece, -1),
        preferred_element_type=jnp.float32,
    ).astype(jnp.bfloat16)
    terms = lax.all_to_all(send, REP, split_axis=0, concat_axis=0, tiled=True)
    summed = jnp.sum(terms.astype(jnp.float32), axis=0).astype(jnp.bfloat16)
    near_cols = summed[: 2 * span].reshape(2 * span, rows_z, piece)
    far_cols = swap_core(summed[2 * span :]).reshape(2 * span, rows_z, piece)
    first = jnp.where(core == 0, near_cols, far_cols)
    second = jnp.where(core == 0, far_cols, near_cols)
    attn_out = jnp.stack([first, second], axis=2).reshape(2, 1, 2, blk, -1)
    new_cache = settle_pages(cache_pages, move_page, arrived)
    return (attn_out, new_cache)


def solution(mesh):
    ctx, rep = mesh.devices.shape
    fine = Mesh(mesh.devices.reshape(rep, ctx // rep // 2, 2, 2, rep // 2), CTX + REP)
    return jax.shard_map(
        on_device,
        mesh=fine,
        in_specs=(
            P(None, CTX, None, None, None),
            P(),
            P(CTX, REP),
            P(CTX, None),
            P(CTX, None),
            P(REP, CTX),
            P(),
            P(),
            P(CTX, REP, None, None, None),
            P(CTX, REP, None),
            P(CTX, REP, None),
            P(CTX, REP, None),
        ),
        out_specs=(P(None, CTX, None, None, REP), P(CTX, REP, None, None, None)),
        check_vma=False,
    )
```

```python
import math

import jax
import jax.numpy as jnp
from jax import lax
from jax.experimental import pallas as pl
from jax.experimental.pallas import tpu as pltpu
from jax.sharding import Mesh
from jax.sharding import PartitionSpec as P

HEAD_SIZE = 128
HEADS_PER_KV = 8

CTX = ("y", "zh", "core")
REP = ("zl", "x")
CHIPS = ("y", "zh")

rope_base = 5000000.0
neg_fill = -1e30


def rope_tables(positions):
    half = HEAD_SIZE // 2
    steps_f = jnp.arange(half, dtype=jnp.float32) * (2.0 / HEAD_SIZE)
    freq = jnp.exp(-steps_f * math.log(rope_base))
    angle = positions.astype(jnp.float32)[:, None] * freq[None, :]
    return (jnp.cos(angle), jnp.sin(angle))


def apply_rotation(values, cosine_table, sine_table):
    half = values.shape[-1] // 2
    first = values[..., :half]
    second = values[..., half:]
    cosine_table = cosine_table[:, None, :]
    sine_table = sine_table[:, None, :]
    return jnp.concatenate(
        [first * cosine_table - second * sine_table, second * cosine_table + first * sine_table],
        axis=-1,
    )


def matmul(left, right):
    return jnp.dot(left, right, preferred_element_type=jnp.float32)


def spread(block, axes):
    size = lax.axis_size(axes)
    copies = jnp.broadcast_to(block[None], (size,) + block.shape)
    return lax.all_to_all(copies, axes, split_axis=0, concat_axis=0, tiled=True)


def swap_core(value):
    return lax.ppermute(value, "core", [(0, 1), (1, 0)])


def swap_x(value):
    return lax.ppermute(value, "x", [(i, i ^ 1) for i in range(lax.axis_size("x"))])


def norm_kernel(core_ref, hidden_ref, gain_ref, near_ref, far_ref):
    hidden = hidden_ref[...].astype(jnp.float32)
    scale = lax.rsqrt(jnp.mean(hidden * hidden, axis=-1, keepdims=True) + 1e-05)
    normed = hidden * scale * gain_ref[...].astype(jnp.float32)
    core = core_ref[0]
    lane = lax.broadcasted_iota(jnp.int32, (hidden.shape[0], 128), 1)
    for pair in range(hidden.shape[1] // 256):
        left = normed[:, 256 * pair : 256 * pair + 128]
        right = normed[:, 256 * pair + 128 : 256 * pair + 256]
        even = jnp.where(lane < 64, left, pltpu.roll(right, 64, 1)).astype(jnp.bfloat16)
        odd = jnp.where(lane < 64, pltpu.roll(left, 64, 1), right).astype(jnp.bfloat16)
        span = slice(128 * pair, 128 * pair + 128)
        near_ref[:, span] = jnp.where(core == 0, even, odd)
        far_ref[:, span] = jnp.where(core == 0, odd, even)


def split_norm(hidden, gain, core):
    rows, width = hidden.shape
    tile = 32
    half = jax.ShapeDtypeStruct((rows, width // 2), jnp.bfloat16)
    half_spec = pl.BlockSpec((tile, width // 2), lambda i: (i, 0))
    return pl.pallas_call(
        norm_kernel,
        grid=(rows // tile,),
        in_specs=[
            pl.BlockSpec(memory_space=pltpu.SMEM),
            pl.BlockSpec((tile, width), lambda i: (i, 0)),
            pl.BlockSpec((1, width), lambda i: (0, 0)),
        ],
        out_specs=(half_spec, half_spec),
        out_shape=(half, half),
        compiler_params=pltpu.CompilerParams(vmem_limit_bytes=12 << 20),
        name="split_norm",
    )(core.reshape(1), hidden, gain[None])


def attend_kernel(q_ref, near_ref, far_ref, qpos_ref, kpos_ref, out_ref):
    half = near_ref.shape[0]
    queries = q_ref[...]
    scores = []
    masks = []
    for part, ref in enumerate((near_ref, far_ref)):
        keys = ref[:, :HEAD_SIZE]
        raw = lax.dot_general(
            queries, keys, (((1,), (1,)), ((), ())), preferred_element_type=jnp.float32
        )
        raw = raw * HEAD_SIZE ** (-0.5)
        allowed = kpos_ref[:, part * half : (part + 1) * half] <= qpos_ref[...]
        scores.append(raw)
        masks.append(allowed)
    top = jnp.maximum(
        jnp.max(jnp.where(masks[0], scores[0], neg_fill), axis=-1, keepdims=True),
        jnp.max(jnp.where(masks[1], scores[1], neg_fill), axis=-1, keepdims=True),
    )
    total = jnp.zeros_like(top)
    acc = jnp.zeros(out_ref.shape, jnp.float32)
    for raw, allowed, ref in zip(scores, masks, (near_ref, far_ref)):
        weights = jnp.where(allowed, jnp.exp(raw - top), 0.0)
        total = total + jnp.sum(weights, axis=-1, keepdims=True)
        acc = acc + matmul(weights.astype(jnp.bfloat16), ref[:, HEAD_SIZE:])
    out_ref[...] = (acc / jnp.maximum(total, 1.0)).astype(jnp.bfloat16)


def attend(queries, near, far, qpos, kpos):
    rows, half = queries.shape[0], near.shape[0]
    tile = min(rows, 128)
    return pl.pallas_call(
        attend_kernel,
        grid=(rows // tile,),
        in_specs=[
            pl.BlockSpec((tile, HEAD_SIZE), lambda i: (i, 0)),
            pl.BlockSpec((half, 2 * HEAD_SIZE), lambda i: (0, 0)),
            pl.BlockSpec((half, 2 * HEAD_SIZE), lambda i: (0, 0)),
            pl.BlockSpec((tile, 1), lambda i: (i, 0)),
            pl.BlockSpec((1, 2 * half), lambda i: (0, 0)),
        ],
        out_specs=pl.BlockSpec((tile, HEAD_SIZE), lambda i: (i, 0)),
        out_shape=jax.ShapeDtypeStruct((rows, HEAD_SIZE), jnp.bfloat16),
        compiler_params=pltpu.CompilerParams(vmem_limit_bytes=40 << 20),
        name="attend",
    )(queries, near, far, qpos, kpos)


def project_kernel(context_ref, weight_ref, out_ref, turned_ref):
    @pl.when(pl.program_id(0) == 0)
    def _():
        turned_ref[...] = context_ref[...].astype(jnp.float32).T.astype(jnp.bfloat16)

    product = jnp.dot(weight_ref[...], turned_ref[...], preferred_element_type=jnp.float32)
    out_ref[...] = product.astype(jnp.bfloat16).reshape(out_ref.shape)


def project(context, weight, groups):
    rows, width = context.shape
    cols = weight.shape[0] // groups
    step = 2
    return pl.pallas_call(
        project_kernel,
        grid=(groups // step,),
        in_specs=[
            pl.BlockSpec((rows, width), lambda i: (0, 0)),
            pl.BlockSpec((step * cols, width), lambda i: (i, 0)),
        ],
        out_specs=pl.BlockSpec((step, cols, rows), lambda i: (i, 0, 0)),
        out_shape=jax.ShapeDtypeStruct((groups, cols, rows), jnp.bfloat16),
        scratch_shapes=[pltpu.VMEM((width, rows), jnp.bfloat16)],
        name="project",
    )(context, weight)


def pages_kernel(page_ref, dest_ref, slot_ref, cache_ref, send_ref):
    groups, moves = send_ref.shape[:2]
    free = cache_ref.shape[0] - moves
    leaving = [cache_ref[page_ref[move]] for move in range(moves)]
    for group in range(groups):
        for slot in range(moves):
            page = jnp.zeros_like(leaving[0])
            for move in range(moves):
                here = (dest_ref[move] == group) & (slot_ref[move] == free + slot)
                page = jnp.where(here, leaving[move], page)
            send_ref[group, slot] = page


def pages_to_send(cache_pages, move_page, move_dest, move_slot):
    pages = cache_pages[0, 0]
    shape = (lax.axis_size(REP), move_page.shape[2]) + pages.shape[1:]
    scalars = pl.BlockSpec(memory_space=pltpu.SMEM)
    vector = pl.BlockSpec(memory_space=pltpu.VMEM)
    return pl.pallas_call(
        pages_kernel,
        in_specs=[scalars, scalars, scalars, vector],
        out_specs=vector,
        out_shape=jax.ShapeDtypeStruct(shape, pages.dtype),
        compiler_params=pltpu.CompilerParams(vmem_limit_bytes=12 << 20),
        name="pages_to_send",
    )(move_page[0, 0], move_dest[0, 0], move_slot[0, 0], pages)


def settle_pages(cache_pages, move_page, arrived):
    pages = cache_pages[0, 0]
    page_count = pages.shape[0]
    moves = move_page.shape[2]
    leave_ids = move_page[0, 0]
    gone = jnp.any(leave_ids[:, None] == jnp.arange(page_count, dtype=jnp.int32)[None, :], axis=0)
    kept = jnp.where(gone[:, None, None], jnp.zeros_like(pages), pages)
    new_pages = jnp.concatenate([kept[: page_count - moves], arrived[0]], axis=0)
    return new_pages.reshape(cache_pages.shape)


def on_device(
    hidden_in,
    norm_gain,
    w_query,
    key_matrix,
    value_matrix,
    w_out,
    prompt_len,
    pair_of_device,
    cache_pages,
    move_page,
    move_dest,
    move_slot,
):
    cycle = lax.axis_size(CTX)
    place = lax.axis_index(CTX)
    rank = lax.axis_index(REP)
    core = lax.axis_index("core")
    rows_y, rows_z = lax.axis_size("y"), lax.axis_size("zh")
    mine = lax.axis_index("x") % 2
    blk = hidden_in.shape[3]
    span = 2 * blk
    width = hidden_in.shape[4]
    piece = w_query.shape[0]
    heads_here = w_query.shape[1] // HEAD_SIZE
    kv_first = (rank * heads_here // HEADS_PER_KV) * HEAD_SIZE

    key_cols = lax.dynamic_slice_in_dim(key_matrix, kv_first, HEAD_SIZE, 1)
    value_cols = lax.dynamic_slice_in_dim(value_matrix, kv_first, HEAD_SIZE, 1)
    half_near = jnp.where(mine == 0, key_cols, value_cols)
    weights = jnp.concatenate([w_query, w_out.T, half_near], axis=1)
    weights = lax.all_gather(weights, "zh", axis=0, tiled=True)
    weights, leave = lax.optimization_barrier((weights, move_page))
    cols = w_query.shape[1]
    wq_near, wo_near = weights[:, :cols], weights[:, cols : 2 * cols]
    half_near = spread(weights[:, 2 * cols :], "y").reshape(-1, HEAD_SIZE)
    wq_near = lax.all_gather(wq_near, "y", axis=0, tiled=True)

    x_near, x_far = split_norm(hidden_in.reshape(2 * span, width), norm_gain, core)
    send_pages = pages_to_send(cache_pages, leave, move_dest, move_slot)
    arrived = lax.psum_scatter(send_pages, REP, scatter_dimension=0, tiled=True)
    x_other = swap_core(x_far)
    half_near, x_near, x_far, wo_near = lax.optimization_barrier(
        (half_near, x_near, x_far, wo_near)
    )
    wo_near = lax.all_gather(wo_near, "y", axis=0, tiled=True)
    half_far = swap_core(half_near)
    x_chip = jnp.concatenate([x_near, x_other], axis=0)

    own_pair = lax.dynamic_slice_in_dim(pair_of_device, place, 1, 1)[:, 0]
    blocks = jnp.stack([own_pair, 2 * cycle - 1 - own_pair], axis=1)
    qpos = (blocks[:, :, None] * blk + jnp.arange(blk, dtype=jnp.int32)).reshape(2, span)
    cosine_table, sine_table = rope_tables(qpos.reshape(-1))

    half = matmul(x_near, half_near) + matmul(x_far, half_far)
    keys = apply_rotation(half[:, None, :], cosine_table, sine_table)[:, 0]
    half = jnp.where(mine == 0, keys, half).astype(jnp.bfloat16).reshape(2, span, HEAD_SIZE)
    kept = lax.dynamic_index_in_dim(half, mine, 0, False)
    other = swap_x(lax.dynamic_index_in_dim(half, 1 - mine, 0, False))
    kv = jnp.where(
        mine == 0,
        jnp.concatenate([kept, other], axis=1),
        jnp.concatenate([other, kept], axis=1),
    )
    kv, x_chip = lax.optimization_barrier((kv, x_chip))
    near = spread(kv, CHIPS).reshape(-1, 2 * HEAD_SIZE)
    query = matmul(x_chip, wq_near)
    query = query[: 2 * span] + swap_core(query[2 * span :])
    query = apply_rotation(
        query.reshape(2 * span, heads_here, HEAD_SIZE), cosine_table, sine_table
    ).astype(jnp.bfloat16)
    query = query.reshape(2, span, heads_here * HEAD_SIZE)
    q_mine = lax.dynamic_index_in_dim(query, mine, 0, False)
    q_pair = swap_x(lax.dynamic_index_in_dim(query, 1 - mine, 0, False))

    pairs = lax.dynamic_index_in_dim(pair_of_device, mine, 0, False).reshape(-1, 2)
    pairs = jnp.where(core == 0, pairs, pairs[:, ::-1]).T.reshape(-1)
    kblocks = jnp.stack([pairs, 2 * cycle - 1 - pairs], axis=1)
    kpos = (kblocks[..., None] * blk + jnp.arange(blk, dtype=jnp.int32)).reshape(1, -1)
    my_qpos = lax.dynamic_index_in_dim(qpos, mine, 0, False)
    my_len = lax.dynamic_index_in_dim(prompt_len, mine, 0, False)
    my_qpos = jnp.where(my_qpos < my_len, my_qpos, -1)
    all_q = jnp.stack([q_mine, q_pair]).reshape(-1, HEAD_SIZE)
    near, all_q, arrived = lax.optimization_barrier((near, all_q, arrived))
    far = swap_core(near)
    all_qpos = jnp.broadcast_to(my_qpos[None, :, None], (2, span, heads_here)).reshape(-1, 1)
    context = attend(all_q, near, far, all_qpos, kpos).reshape(2, span, heads_here * HEAD_SIZE)
    c_pair = swap_x(context[1])
    c_mine = context[0]
    context = jnp.concatenate(
        [jnp.where(mine == 0, c_mine, c_pair), jnp.where(mine == 0, c_pair, c_mine)], axis=0
    )
    context = jnp.concatenate([context, swap_core(context)], axis=0)
    context, wo_near = lax.optimization_barrier((context, wo_near))
    send = project(context, wo_near, rows_y)
    terms = lax.all_to_all(send, REP, split_axis=0, concat_axis=0, tiled=True)
    terms = jnp.swapaxes(terms, 1, 2)
    summed = jnp.sum(terms.astype(jnp.float32), axis=0).astype(jnp.bfloat16)
    near_cols = summed[: 2 * span].reshape(2 * span, rows_z, piece)
    far_cols = swap_core(summed[2 * span :]).reshape(2 * span, rows_z, piece)
    first = jnp.where(core == 0, near_cols, far_cols)
    second = jnp.where(core == 0, far_cols, near_cols)
    attn_out = jnp.stack([first, second], axis=2).reshape(2, 1, 2, blk, -1)
    new_cache = settle_pages(cache_pages, move_page, arrived)
    return (attn_out, new_cache)


def solution(mesh):
    ctx, rep = mesh.devices.shape
    fine = Mesh(mesh.devices.reshape(rep, ctx // rep // 2, 2, 2, rep // 2), CTX + REP)
    return jax.shard_map(
        on_device,
        mesh=fine,
        in_specs=(
            P(None, CTX, None, None, None),
            P(),
            P(CTX, REP),
            P(CTX, None),
            P(CTX, None),
            P(REP, CTX),
            P(),
            P(),
            P(CTX, REP, None, None, None),
            P(CTX, REP, None),
            P(CTX, REP, None),
            P(CTX, REP, None),
        ),
        out_specs=(P(None, CTX, None, None, REP), P(CTX, REP, None, None, None)),
        check_vma=False,
    )
```
